512 devices in a mesh: cell: 64 (over y, x, z_lo), gene: 8 (over z_hi, core).
Axes of the slice: x: 4, y: 4, z: 16 (z_hi: 4, z_lo: 4; z = z_hi * 4 + z_lo), core: 2. Of those that a mesh axis runs over, the one named last changes fastest.
Arguments:
- counts: int32 [8192, 32768], P('cell', 'gene'), may hold values from 0 to 3
- size_factor: int32 [8192], P('cell'), may hold values from 1200 to 2400
- gene_offset: float32 [32768], P('gene'), may hold values from -1.5 to 0.5
- factors: float32 [32, 8192], P(None, 'cell'), may hold values from -1.5 to 1.5
- loadings: float32 [32, 8, 4096], P(None, 'gene', 'cell'), may hold values from -1.5 to 1.5
Outputs:
- factors_next: float32 [32, 8192], P(None, 'cell')
- loadings_next: float32 [32, 8, 4096], P(None, 'gene', 'cell')
The draws below stay inside these ranges and needn't reach their ends.
All inputs are finite; a program needn't handle non-finite values.
Results may differ from the reference program's by a relative error of at most 0.0003.
Values sent between devices are 32-bit elements; how exact they have to be, the bound alone decides.
A program may use at most 64 MiB of HBM per device.

```python
import math
import jax
import jax.numpy as jnp
from jax import lax

RANK = 32
GENES = 32768
ITERS = 2
FACTOR_STEPS = 4
CELLS = 8192
GROUPS = 8
SLAB = 4096


def set_ends(drawn, stream_key, smallest, top_value):
    index_at = [jax.random.randint(jax.random.fold_in(stream_key, axis), (), 0, length) for axis, length in enumerate(drawn.shape)]
    main_axis = drawn.shape.index(max(drawn.shape))
    neighbour = index_at[:main_axis] + [(index_at[main_axis] + 1) % drawn.shape[main_axis]] + index_at[main_axis + 1:]
    return drawn.at[tuple(index_at)].set(smallest).at[tuple(neighbour)].set(top_value)


def levels(own_key, extent, pieces, smallest, top_value):
    gain = 1.0
    for position, shards_of in pieces:
        steps = jax.random.uniform(jax.random.fold_in(jax.random.fold_in(own_key, 6), position), (shards_of,), jnp.float32, smallest / len(pieces), top_value / len(pieces))
        gain = gain * jnp.repeat(jnp.exp(steps), extent[position] // shards_of).reshape((-1,) + (1,) * (len(extent) - 1 - position))
    return gain


def noise(own_key, shape, scale, limit, cuts=(), kind=jnp.bfloat16):
    level = levels(own_key, shape, cuts, -0.22, 0.18) if cuts else 1.0
    values = jax.random.normal(own_key, shape, jnp.float32) * scale * level
    return jnp.minimum(jnp.maximum(values, -limit), limit).astype(kind)


def setup_inputs(seed: int = 0) -> dict:
    seeds = jax.random.split(jax.random.key(seed), 6)
    return {
        "counts": set_ends(jax.random.randint(seeds[0], (CELLS, GENES), 0, 4), jax.random.fold_in(seeds[0], 1), 0, 3).astype(jnp.int32),
        "size_factor": set_ends(jax.random.randint(seeds[1], (CELLS,), 1200, 2401), jax.random.fold_in(seeds[1], 1), 1200, 2400).astype(jnp.int32),
        "gene_offset": jnp.clip(-1.5 + 2.0 * jax.random.uniform(seeds[2], (GENES,), jnp.float32) ** levels(seeds[2], (GENES,), ((0, 8),), -0.2, 0.2), -1.5, 0.5),
        "factors": noise(seeds[3], (RANK, CELLS), 0.25, 1.5, ((1, 64),), jnp.float32),
        "loadings": noise(seeds[4], (RANK, GROUPS, SLAB), 0.25, 1.5, ((1, 8), (2, 64)), jnp.float32),
    }


HIGH = lax.Precision.HIGHEST

def shrink(values, level):
    kept = jnp.maximum(jnp.abs(values) - level, 0.0)
    return jnp.sign(values) * kept / 1.1

def reference(counts, size_factor, gene_offset, factors, loadings):
    block = math.gcd(CELLS, 1024)
    nblock = CELLS // block
    offset = jnp.log(size_factor.astype(jnp.float32) / 2000.0)
    current = factors
    whole = loadings.reshape(RANK, GENES)
    count_blocks = counts.reshape(nblock, block, GENES)
    offset_blocks = offset.reshape(nblock, block)
    eye = jnp.eye(RANK, dtype=jnp.float32)
    for step in range(ITERS):
        gram_u = jnp.dot(current, current.T, precision=HIGH)
        gram_v = jnp.dot(whole, whole.T, precision=HIGH)
        hess = gram_v + 0.1 * (jnp.trace(gram_v) / RANK) * eye
        chol = jnp.linalg.cholesky(hess)
        factor_blocks = current.reshape(RANK, nblock, block).transpose(1, 0, 2)

        def visit(carry, items):
            count_blk, offset_blk, factor_blk = items
            observed = count_blk.astype(jnp.float32)

            def resid_of(factor_now):
                eta = offset_blk[:, None] + gene_offset[None, :] + lax.dot_general(factor_now, whole, (((0,), (0,)), ((), ())), precision=HIGH)
                return jnp.exp(eta) - observed
            resid = resid_of(factor_blk)
            carry = carry + jnp.dot(factor_blk, resid, precision=HIGH)
            for turn in range(FACTOR_STEPS):
                if turn > 0:
                    resid = resid_of(factor_blk)
                grad_blk = lax.dot_general(whole, resid, (((1,), (1,)), ((), ())), precision=HIGH)
                factor_blk = factor_blk - 0.25 * jax.scipy.linalg.cho_solve((chol, True), grad_blk)
            return (carry, factor_blk)
        grad_v, new_blocks = lax.scan(visit, jnp.zeros((RANK, GENES), jnp.float32), (count_blocks, offset_blocks, factor_blocks))
        current = new_blocks.transpose(1, 0, 2).reshape(RANK, CELLS)
        rate = 0.5 * RANK / jnp.trace(gram_u)
        level = 0.1 * jnp.sqrt(jnp.trace(gram_v) / (RANK * GENES) + 1e-06)
        whole = shrink(whole - rate * grad_v, level)
    return (current, whole.reshape(RANK, GROUPS, SLAB))
```

```python
import functools

import jax
import jax.numpy as jnp
from jax import lax
from jax.experimental import pallas as pl
from jax.experimental.pallas import tpu as pltpu
from jax.sharding import PartitionSpec as P

ITERS = 2
FACTOR_STEPS = 4
RANK = 32
MESH = pl.DeviceIdType.MESH
F32 = jnp.float32
BF16 = jnp.bfloat16
HIGH = lax.Precision.HIGHEST
SPLITS = {64: (4, 4, 4), 8: (2, 2, 2)}


def split2(value):
    high = value.astype(BF16)
    return high, (value - high.astype(F32)).astype(BF16)


def split3(value):
    first = value.astype(BF16).astype(F32)
    rest = value - first
    second = rest.astype(BF16).astype(F32)
    return first, second, rest - second


def kernel(dims, cnt_hbm, sf_ref, goff_ref, u_ref, vv_ref, uo_ref, vo_ref,
           cnt, gop, zbuf, vb, vst, rb, gp, prs, ra1, rb1, a1, b1, ra2, rb2, rz, vnew, trb, arb, grb, upb,
           s_local, s_cnt, r_cnt, s_go, r_go, s_z, r_z, s_ag, r_ag, s_rs, r_rs, s_tr, r_tr, s_ar, r_ar, s_gr, r_gr,
           s_uf, r_uf):
    ny, nx, nz, nh = dims
    bx = nz * 64
    by = nx * bx
    nch = 2 * ny
    genes = 2 * nh * ny * by
    p = lax.axis_index("cell")
    q = lax.axis_index("gene")
    z = lax.rem(p, nz)
    x = lax.rem(p // nz, nx)
    y = p // (nz * nx)
    core = lax.rem(q, 2)
    h = q // 2

    def to_x(i):
        return {"cell": y * (nx * nz) + i * nz + z, "gene": q}

    def to_y(i):
        return {"cell": i * (nx * nz) + x * nz + z, "gene": q}

    def to_z(i):
        return {"cell": y * (nx * nz) + x * nz + i, "gene": q}

    def to_h(i):
        return {"cell": p, "gene": i * 2 + core}

    pair = {"cell": p, "gene": h * 2 + 1 - core}
    axes = {"x": (to_x, x, nx), "y": (to_y, y, ny), "z": (to_z, z, nz), "h": (to_h, h, nh)}
    pending = []

    def remote(src, dst, send, recv, device):
        return pltpu.make_async_remote_copy(
            src_ref=src, dst_ref=dst, send_sem=send, recv_sem=recv, device_id=device, device_id_type=MESH)

    def send_all(axis, source, target, send, recv):
        to, me, n = axes[axis]
        for k in range(1, n):
            i = lax.rem(me + k, n)
            copy = remote(source(i), target(me), send(k), recv(k), to(i))
            copy.start()
            pending.append(copy)

    def recv_all(axis, target, send, recv):
        to, me, n = axes[axis]
        for k in range(1, n):
            i = lax.rem(me + n - k, n)
            remote(target(i), target(i), send(k), recv(k), to(i)).wait_recv()

    def send_pair(src, dst, send, recv):
        copy = remote(src, dst, send, recv, pair)
        copy.start()
        pending.append(copy)
        return copy

    lane = lax.broadcasted_iota(jnp.int32, (RANK, 128), 1)
    row = lax.broadcasted_iota(jnp.int32, (RANK, 128), 0)
    low16 = lane[0:16] < 64

    barrier = pltpu.get_barrier_semaphore()
    partners = 1
    pl.semaphore_signal(barrier, inc=1, device_id=pair, device_id_type=MESH)
    for to, me, n in axes.values():
        for k in range(1, n):
            pl.semaphore_signal(barrier, inc=1, device_id=to(lax.rem(me + k, n)), device_id_type=MESH)
            partners += 1
    local = []
    for j in range(ny):
        copy = pltpu.make_async_copy(
            cnt_hbm.at[pl.ds(pl.multiple_of(core * 64, 64), 64), pl.ds(j * by, by)], cnt.at[j], s_local.at[j])
        copy.start()
        local.append(copy)
    zbuf[z] = jnp.where((lane >= 64) == (lax.rem(z, 2) == 1), vv_ref[...], 0.0)
    pl.semaphore_wait(barrier, partners)

    send_all("z", lambda i: zbuf.at[z], lambda i: zbuf.at[i], lambda k: s_z.at[k], lambda k: r_z.at[k])
    go_copy = send_pair(goff_ref, gop, s_go.at[0], r_go.at[0])
    cnt_copies = []
    for j in range(ny):
        cnt_copies.append(send_pair(
            cnt_hbm.at[pl.ds(pl.multiple_of((1 - core) * 64, 64), 64), pl.ds(j * by, by)], cnt.at[ny + j],
            s_cnt.at[j], r_cnt.at[j]))

    xs = pl.ds(pl.multiple_of(x * bx, 128), bx)

    def xcols(i):
        return pl.ds(pl.multiple_of(i * bx, 128), bx)

    top, bottom = pl.ds(0, 16), pl.ds(16, 16)

    def sem(array, it, stage):
        return lambda k: array.at[it, stage, k]

    def gather_first(it):
        send_all("x", lambda i: vb.at[it, 0, y, top, xs], lambda i: vb.at[it, 0, y, top, xcols(i)],
                 sem(s_ag, it, 0), sem(r_ag, it, 0))
        send_all("y", lambda i: vb.at[it, 0, y, bottom, xs], lambda i: vb.at[it, 0, i, bottom, xs],
                 sem(s_ag, it, 1), sem(r_ag, it, 1))

    def gather_second(it):
        recv_all("x", lambda i: vb.at[it, 0, y, top, xcols(i)], sem(s_ag, it, 0), sem(r_ag, it, 0))
        send_all("y", lambda i: vb.at[it, 0, y, top, :], lambda i: vb.at[it, 0, i, top, :],
                 sem(s_ag, it, 2), sem(r_ag, it, 2))
        recv_all("y", lambda i: vb.at[it, 0, i, bottom, xs], sem(s_ag, it, 1), sem(r_ag, it, 1))
        send_all("x", lambda i: vb.at[it, 0, :, bottom, xs], lambda i: vb.at[it, 0, :, bottom, xcols(i)],
                 sem(s_ag, it, 3), sem(r_ag, it, 3))

    def gather_third(it):
        recv_all("y", lambda i: vb.at[it, 0, i, top, :], sem(s_ag, it, 2), sem(r_ag, it, 2))
        recv_all("x", lambda i: vb.at[it, 0, :, bottom, xcols(i)], sem(s_ag, it, 3), sem(r_ag, it, 3))
        return send_pair(vb.at[it, 0], vb.at[it, 1], s_ag.at[it, 4, 0], r_ag.at[it, 4, 0])

    def stack_slot(it, slot):
        def one(j, carry):
            high, low = split2(vb[it, slot, j])
            chunk = slot * ny + j
            vst[it, chunk, 0:32] = high
            vst[it, chunk, 32:64] = low
            vst[it, chunk, 64:96] = high
            return carry
        lax.fori_loop(0, ny, one, 0)

    def extra_slot(slot, ref):
        rows = lax.broadcasted_iota(jnp.int32, (RANK, by), 0)
        for j in range(ny):
            g1, g2, g3 = split3(ref[:, j * by:(j + 1) * by])
            extra = jnp.where(rows < 3, 1.0, jnp.where(rows == 3, g1, jnp.where(rows == 4, g2, jnp.where(rows == 5, g3, 0.0))))
            extra = extra.astype(BF16)
            for it in range(ITERS):
                vst[it, slot * ny + j, 96:128] = extra

    def gram_send(it):
        def one(chunk, acc):
            w = vst[it, chunk]
            return acc + lax.dot_general(w[0:64], w, (((1,), (1,)), ((), ())), preferred_element_type=F32)
        acc = lax.fori_loop(0, nch, one, jnp.zeros((64, 128), F32))
        both = acc[0:32] + acc[32:64]
        gram = both + pltpu.roll(both, 96, 1)
        small = lane[0:8]
        packed = jnp.where(small < 32, gram[0:8], jnp.where(
            small < 64, pltpu.roll(gram[8:16], 32, 1), jnp.where(
                small < 96, pltpu.roll(gram[16:24], 64, 1), pltpu.roll(gram[24:32], 96, 1))))
        grb[it, h] = packed
        send_all("h", lambda i: grb.at[it, h], lambda i: grb.at[it, i], lambda k: s_gr.at[it, k], lambda k: r_gr.at[it, k])

    def gram_finish(it):
        recv_all("h", lambda i: grb.at[it, i], lambda k: s_gr.at[it, k], lambda k: r_gr.at[it, k])
        total = grb[it, 0]
        for i in range(1, nh):
            total = total + grb[it, i]
        gram = jnp.concatenate([total] + [pltpu.roll(total, 128 - 32 * i, 1) for i in range(1, 4)], axis=0)
        gram = jnp.where(lane < 32, gram, 0.0)
        diagonal = row == lane
        trace = jnp.sum(jnp.sum(jnp.where(diagonal, gram, 0.0), axis=1, keepdims=True), axis=0, keepdims=True)
        hess = gram + jnp.where(diagonal, 0.1 * (trace / RANK), 0.0)

        def pivot(k, a):
            rmask = row == k
            lmask = lane == k
            prow = jnp.sum(jnp.where(rmask, a, 0.0), axis=0, keepdims=True)
            pcol = jnp.sum(jnp.where(lmask, a, 0.0), axis=1, keepdims=True)
            d = jnp.sum(jnp.where(rmask[:, 0:1], pcol, 0.0), axis=0, keepdims=True)
            inv = 1.0 / d
            scaled = jnp.where(lmask[0:1], inv, prow * inv)
            rest = jnp.where(lmask, 0.0, a) - jnp.where(rmask[:, 0:1], 0.0, pcol) * scaled
            return jnp.where(rmask, scaled, rest)
        inverse = lax.fori_loop(0, RANK, pivot, hess)
        return trace, 0.25 * inverse[:, 0:RANK]

    sf = jnp.log(sf_ref[...].astype(F32) / 2000.0)
    sf = jnp.where(core == 0, sf, pltpu.roll(sf, 64, 1))
    o1, o2, o3 = split3(sf)
    offrows = jnp.where(row == 0, o1, jnp.where(row == 1, o2, jnp.where(row == 2, o3, jnp.where(row < 6, 1.0, 0.0))))

    def lhs_of(u):
        first = u.astype(BF16).astype(F32)
        stack = jnp.concatenate([first, first, u - first, offrows], axis=0)
        return stack.T[0:64].astype(BF16)

    def grad_partial(it, u, store):
        lhs = lhs_of(u)

        def one(chunk, acc):
            w = vst[it, chunk]
            eta = jnp.dot(lhs, w, preferred_element_type=F32)
            resid = jnp.exp(eta) - cnt[chunk].astype(F32)
            r1, r2 = split2(resid)
            both = jnp.concatenate([r1, r2], axis=0)
            if store:
                rb[chunk] = both
            return acc + lax.dot_general(w[0:64], both, (((1,), (1,)), ((), ())), preferred_element_type=F32)
        acc = lax.fori_loop(0, nch, one, jnp.zeros((64, 128), F32))
        s = acc[0:32] + acc[32:64]
        g = s + pltpu.roll(s, 64, 1)
        return jnp.where(low16, g[0:16], g[16:32])

    def grad_send(n, packed):
        arb[n, h] = packed
        send_all("h", lambda i: arb.at[n, h], lambda i: arb.at[n, i], lambda k: s_ar.at[n, k], lambda k: r_ar.at[n, k])

    def grad_finish(n, u, quarter_inverse):
        recv_all("h", lambda i: arb.at[n, i], lambda k: s_ar.at[n, k], lambda k: r_ar.at[n, k])
        total = arb[n, 0]
        for i in range(1, nh):
            total = total + arb[n, i]
        grad = jnp.concatenate([total, pltpu.roll(total, 64, 1)], axis=0)
        return u - jnp.dot(quarter_inverse, grad, precision=HIGH, preferred_element_type=F32)

    def scatter_start(it, u):
        dup = jnp.where(lane < 64, u, pltpu.roll(u, 64, 1))
        high, low = split2(dup)
        lhs = jnp.concatenate([high, low], axis=0)

        def make(slot):
            def one(j, carry):
                out = jnp.dot(lhs, rb[slot * ny + j], preferred_element_type=F32)
                gp[it, slot, j] = out[0:32] + out[32:64]
                return carry
            lax.fori_loop(0, ny, one, 0)
        make(1)
        first = send_pair(gp.at[it, 1], prs.at[it], s_rs.at[it, 0, 0], r_rs.at[it, 0, 0])
        square = jnp.where(lane < 64, u * u, 0.0)
        square = jnp.sum(jnp.sum(square, axis=1, keepdims=True), axis=0, keepdims=True)
        trb[it, 0, 0] = jnp.broadcast_to(square, (8, 128))
        second = send_pair(trb.at[it, 0, 0], trb.at[it, 0, 1], s_tr.at[it, 0, 0], r_tr.at[it, 0, 0])
        make(0)
        return first, second

    def trace_stage(it, axis, stage, value):
        _, me, _ = axes[axis]
        trb[it, stage, me] = value
        send_all(axis, lambda i: trb.at[it, stage, me], lambda i: trb.at[it, stage, i],
                 sem(s_tr, it, stage), sem(r_tr, it, stage))

    def trace_sum(it, axis, stage):
        _, _, n = axes[axis]
        recv_all(axis, lambda i: trb.at[it, stage, i], sem(s_tr, it, stage), sem(r_tr, it, stage))
        total = trb[it, stage, 0]
        for i in range(1, n):
            total = total + trb[it, stage, i]
        return total

    def scatter_first(it, copies):
        copies[1].wait_recv()
        trace_stage(it, "y", 1, trb[it, 0, 0] + trb[it, 0, 1])
        copies[0].wait_recv()

        def one(j, carry):
            gp[it, 0, j] += prs[it, j]
            return carry
        lax.fori_loop(0, ny, one, 0)
        send_all("y", lambda i: gp.at[it, 0, i, top, :], lambda i: ra1.at[it, i], sem(s_rs, it, 1), sem(r_rs, it, 1))
        send_all("x", lambda i: gp.at[it, 0, :, bottom, xcols(i)], lambda i: rb1.at[it, i], sem(s_rs, it, 2), sem(r_rs, it, 2))
        ra1[it, y] = gp[it, 0, y, 0:16, :]
        rb1[it, x] = gp[it, 0, :, 16:32, xs]

    def scatter_second(it):
        trace_stage(it, "x", 2, trace_sum(it, "y", 1))
        recv_all("y", lambda i: ra1.at[it, i], sem(s_rs, it, 1), sem(r_rs, it, 1))
        total = ra1[it, 0]
        for i in range(1, ny):
            total = total + ra1[it, i]
        a1[it] = total
        send_all("x", lambda i: a1.at[it, :, xcols(i)], lambda i: ra2.at[it, i], sem(s_rs, it, 3), sem(r_rs, it, 3))
        recv_all("x", lambda i: rb1.at[it, i], sem(s_rs, it, 2), sem(r_rs, it, 2))
        total = rb1[it, 0]
        for i in range(1, nx):
            total = total + rb1[it, i]
        b1[it] = total
        send_all("y", lambda i: b1.at[it, i], lambda i: rb2.at[it, i], sem(s_rs, it, 4), sem(r_rs, it, 4))
        ra2[it, x] = a1[it, :, xs]
        rb2[it, y] = b1[it, y]

    def scatter_third(it):
        trace_stage(it, "z", 3, trace_sum(it, "x", 2))
        recv_all("x", lambda i: ra2.at[it, i], sem(s_rs, it, 3), sem(r_rs, it, 3))
        recv_all("y", lambda i: rb2.at[it, i], sem(s_rs, it, 4), sem(r_rs, it, 4))
        total = ra2[it, 0]
        for i in range(1, nx):
            total = total + ra2[it, i]
        rz[it, z, 0:16] = total
        total = rb2[it, 0]
        for i in range(1, ny):
            total = total + rb2[it, i]
        rz[it, z, 16:32] = total
        send_all("z", lambda i: rz.at[it, z], lambda i: rz.at[it, i], sem(s_rs, it, 5), sem(r_rs, it, 5))

    def scatter_finish(it, gram_trace):
        trace_u = trace_sum(it, "z", 3)[0:1, 0:1]
        recv_all("z", lambda i: rz.at[it, i], sem(s_rs, it, 5), sem(r_rs, it, 5))
        total = rz[it, 0]
        for i in range(1, nz):
            total = total + rz[it, i]
        rate = (0.5 * RANK) / trace_u
        level = 0.1 * jnp.sqrt(gram_trace / (RANK * genes) + 1e-06)
        w = vb[it, 0, y, :, xs] - rate * total
        return jnp.where(w > level, w - level, jnp.where(w < -level, w + level, 0.0)) / 1.1

    recv_all("z", lambda i: zbuf.at[i], lambda k: s_z.at[k], lambda k: r_z.at[k])
    for t in range(bx // 128):
        vb[0, 0, y, :, pl.ds(pl.multiple_of(x * bx + t * 128, 128), 128)] = zbuf[2 * t] + zbuf[2 * t + 1]
    gather_first(0)
    extra_slot(0, goff_ref)
    go_copy.wait_recv()
    extra_slot(1, gop)
    gather_second(0)
    other = gather_third(0)
    stack_slot(0, 0)
    for copy in local:
        copy.wait()
    for copy in cnt_copies:
        copy.wait_recv()
    other.wait_recv()
    stack_slot(0, 1)

    u = jnp.where(core == 0, u_ref[...], pltpu.roll(u_ref[...], 64, 1))
    for it in range(ITERS):
        start_u = u
        gram_send(it)
        grad_send(4 * it, grad_partial(it, u, True))
        copies = scatter_start(it, start_u)
        gram_trace, quarter_inverse = gram_finish(it)
        u = grad_finish(4 * it, u, quarter_inverse)
        for turn in range(1, FACTOR_STEPS):
            grad_send(4 * it + turn, grad_partial(it, u, False))
            if turn == 1:
                scatter_first(it, copies)
            elif turn == 2:
                scatter_second(it)
            else:
                scatter_third(it)
            u = grad_finish(4 * it + turn, u, quarter_inverse)
        fresh = scatter_finish(it, gram_trace)
        if it < ITERS - 1:
            vb[it + 1, 0, y, :, xs] = fresh
            gather_first(it + 1)
            gather_second(it + 1)
            other = gather_third(it + 1)
            stack_slot(it + 1, 0)
            other.wait_recv()
            stack_slot(it + 1, 1)
        else:
            upb[0] = jnp.where(low16, u[0:16], pltpu.roll(u[16:32], 64, 1))
            last = send_pair(upb.at[0], upb.at[1], s_uf.at[0], r_uf.at[0])
            vnew[...] = fresh
            vo_ref[...] = vnew[:, pl.ds(pl.multiple_of((z // 2) * 128, 128), 128)]
            last.wait_recv()
            theirs = upb[1]
            theirs = jnp.concatenate([theirs, pltpu.roll(theirs, 64, 1)], axis=0)
            mine_first = jnp.where(lane < 64, u, pltpu.roll(theirs, 64, 1))
            theirs_first = jnp.where(lane < 64, theirs, pltpu.roll(u, 64, 1))
            uo_ref[...] = jnp.where(core == 0, mine_first, theirs_first)
    for copy in pending:
        copy.wait_send()


def on_device(dims, counts, size_factor, gene_offset, factors, loadings):
    ny, nx, nz, nh = dims
    bx = nz * 64
    by = nx * bx
    slab = ny * by
    nch = 2 * ny
    most = max(ny, nx, nz, nh)
    shard = loadings.reshape(RANK, 64)
    doubled = jnp.concatenate([shard, shard], axis=1)
    dma = pltpu.SemaphoreType.DMA
    vmem = pl.BlockSpec(memory_space=pltpu.VMEM)
    scratch = [
        pltpu.VMEM((nch, 64, by), jnp.int32),
        pltpu.VMEM((1, slab), F32),
        pltpu.VMEM((nz, RANK, 128), F32),
        pltpu.VMEM((ITERS, 2, ny, RANK, by), F32),
        pltpu.VMEM((ITERS, nch, 128, by), BF16),
        pltpu.VMEM((nch, 128, by), BF16),
        pltpu.VMEM((ITERS, 2, ny, RANK, by), F32),
        pltpu.VMEM((ITERS, ny, RANK, by), F32),
        pltpu.VMEM((ITERS, ny, 16, by), F32),
        pltpu.VMEM((ITERS, nx, ny, 16, bx), F32),
        pltpu.VMEM((ITERS, 16, by), F32),
        pltpu.VMEM((ITERS, ny, 16, bx), F32),
        pltpu.VMEM((ITERS, nx, 16, bx), F32),
        pltpu.VMEM((ITERS, ny, 16, bx), F32),
        pltpu.VMEM((ITERS, nz, RANK, bx), F32),
        pltpu.VMEM((RANK, bx), F32),
        pltpu.VMEM((ITERS, 4, most, 8, 128), F32),
        pltpu.VMEM((ITERS * FACTOR_STEPS, nh, 16, 128), F32),
        pltpu.VMEM((ITERS, nh, 8, 128), F32),
        pltpu.VMEM((2, 16, 128), F32),
        dma((ny,)), dma((ny,)), dma((ny,)), dma((1,)), dma((1,)),
        dma((nz,)), dma((nz,)),
        dma((ITERS, 5, most)), dma((ITERS, 5, most)),
        dma((ITERS, 6, most)), dma((ITERS, 6, most)),
        dma((ITERS, 4, most)), dma((ITERS, 4, most)),
        dma((ITERS * FACTOR_STEPS, nh)), dma((ITERS * FACTOR_STEPS, nh)),
        dma((ITERS, nh)), dma((ITERS, nh)),
        dma((1,)), dma((1,)),
    ]
    u_next, v_next = pl.pallas_call(
        functools.partial(kernel, dims),
        out_shape=(jax.ShapeDtypeStruct((RANK, 128), F32), jax.ShapeDtypeStruct((RANK, 128), F32)),
        in_specs=[pl.BlockSpec(memory_space=pl.ANY), vmem, vmem, vmem, vmem],
        out_specs=(vmem, vmem),
        scratch_shapes=scratch,
        compiler_params=pltpu.CompilerParams(
            collective_id=0, has_side_effects=True, vmem_limit_bytes=48 * 1024 * 1024),
    )(counts, size_factor.reshape(1, 128), gene_offset.reshape(1, slab), factors, doubled)
    odd = lax.rem(lax.axis_index("cell"), 2) == 1
    v_next = jnp.where(odd, v_next[:, 64:], v_next[:, :64])
    return u_next, v_next.reshape(RANK, 1, 64)


def solution(mesh):
    dims = SPLITS[mesh.shape["cell"]] + (mesh.shape["gene"] // 2,)
    return jax.shard_map(
        functools.partial(on_device, dims),
        mesh=mesh,
        in_specs=(
            P("cell", "gene"),
            P("cell"),
            P("gene"),
            P(None, "cell"),
            P(None, "gene", "cell"),
        ),
        out_specs=(P(None, "cell"), P(None, "gene", "cell")),
        check_vma=False,
    )
```

```python
import functools

import jax
import jax.numpy as jnp
from jax import lax
from jax.experimental import pallas as pl
from jax.experimental.pallas import tpu as pltpu
from jax.sharding import PartitionSpec as P

ITERS = 2
FACTOR_STEPS = 4
RANK = 32
MESH = pl.DeviceIdType.MESH
F32 = jnp.float32
BF16 = jnp.bfloat16
HIGH = lax.Precision.HIGHEST
SPLITS = {64: (4, 4, 4), 8: (2, 2, 2)}


def split2(value):
    high = value.astype(BF16)
    return high, (value - high.astype(F32)).astype(BF16)


def split3(value):
    first = value.astype(BF16).astype(F32)
    rest = value - first
    second = rest.astype(BF16).astype(F32)
    return first, second, rest - second


def kernel(dims, cnt_hbm, sf_hbm, goff_hbm, u_hbm, v_hbm, uo_ref, vo_ref,
           sf_ref, goff_ref, u_ref, v_ref, cnt, gop, zbuf, vb, vst, rb, gp, prs, ra1, rb1, a1, b1, ra2, rb2, rz, vnew, trb, arb, grb, gpb, upb,
           s_in, met_ring, met_line, met_far, s_gp, r_gp, s_local, s_cnt, r_cnt, s_go, r_go, s_z, r_z, s_ag, r_ag, s_rs, r_rs, s_tr, r_tr, s_ar, r_ar, s_gr, r_gr,
           s_uf, r_uf):
    ny, nx, nz, nh = dims
    bx = nz * 64
    by = nx * bx
    nch = 2 * ny
    genes = 2 * nh * ny * by
    p = lax.axis_index("cell")
    q = lax.axis_index("gene")
    z = lax.rem(p, nz)
    x = lax.rem(p // nz, nx)
    y = p // (nz * nx)
    core = lax.rem(q, 2)
    h = q // 2

    def to_x(i):
        return {"cell": y * (nx * nz) + i * nz + z, "gene": q}

    def to_y(i):
        return {"cell": i * (nx * nz) + x * nz + z, "gene": q}

    def to_z(i):
        return {"cell": y * (nx * nz) + x * nz + i, "gene": q}

    def to_h(i):
        return {"cell": p, "gene": i * 2 + core}

    pair = {"cell": p, "gene": h * 2 + 1 - core}
    axes = {"x": (to_x, x, nx), "y": (to_y, y, ny), "z": (to_z, z, nz), "h": (to_h, h, nh)}
    pending = []

    def far_first(n):
        return sorted(range(1, n), key=lambda k: -min(k, n - k))

    def near_first(n):
        return sorted(range(1, n), key=lambda k: min(k, n - k))

    def ring(step):
        other = lax.rem(h * nz + z + step + nh * nz, nh * nz)
        return {"cell": y * (nx * nz) + x * nz + lax.rem(other, nz), "gene": (other // nz) * 2 + core}

    def signal(semaphore, device):
        pl.semaphore_signal(semaphore, inc=1, device_id=device, device_id_type=MESH)


    def remote(src, dst, send, recv, device):
        return pltpu.make_async_remote_copy(
            src_ref=src, dst_ref=dst, send_sem=send, recv_sem=recv, device_id=device, device_id_type=MESH)

    def send_all(axis, source, target, send, recv):
        to, me, n = axes[axis]
        for k in far_first(n):
            i = lax.rem(me + k, n)
            copy = remote(source(i), target(me), send(k), recv(k), to(i))
            copy.start()
            pending.append(copy)

    def recv_all(axis, target, send, recv):
        to, me, n = axes[axis]
        for k in range(1, n):
            i = lax.rem(me + n - k, n)
            remote(target(i), target(i), send(k), recv(k), to(i)).wait_recv()

    def send_pair(src, dst, send, recv):
        copy = remote(src, dst, send, recv, pair)
        copy.start()
        pending.append(copy)
        return copy

    lane = lax.broadcasted_iota(jnp.int32, (RANK, 128), 1)
    row = lax.broadcasted_iota(jnp.int32, (RANK, 128), 0)
    low16 = lane[0:16] < 64

    barrier = pltpu.get_barrier_semaphore()
    signal(barrier, pair)
    signal(barrier, ring(1))
    signal(barrier, ring(-1))
    partners = 3
    for axis in ("x", "y", "z"):
        to, me, n = axes[axis]
        for k in range(1, n):
            signal(barrier, to(lax.rem(me + k, n)))
            partners += 1
    inputs = []
    for j, (src, dst) in enumerate(((v_hbm, v_ref), (sf_hbm, sf_ref), (goff_hbm, goff_ref), (u_hbm, u_ref))):
        copy = pltpu.make_async_copy(src, dst, s_in.at[j])
        copy.start()
        inputs.append(copy)
    local = []
    for j in range(ny):
        copy = pltpu.make_async_copy(
            cnt_hbm.at[pl.ds(pl.multiple_of(core * 64, 64), 64), pl.ds(j * by, by)], cnt.at[j], s_local.at[j])
        copy.start()
        local.append(copy)
    inputs[0].wait()
    shard = v_ref[...]
    shard = jnp.concatenate([shard, shard], axis=1)
    zbuf[z] = jnp.where((lane >= 64) == (lax.rem(z, 2) == 1), shard, 0.0)
    pl.semaphore_wait(barrier, partners)

    send_all("z", lambda i: zbuf.at[z], lambda i: zbuf.at[i], lambda k: s_z.at[k], lambda k: r_z.at[k])
    signal(met_ring, ring(1))
    signal(met_ring, ring(-1))
    go_copy = send_pair(goff_hbm, gop, s_go.at[0], r_go.at[0])
    cnt_copies = []
    for j in range(ny):
        cnt_copies.append(send_pair(
            cnt_hbm.at[pl.ds(pl.multiple_of((1 - core) * 64, 64), 64), pl.ds(j * by, by)], cnt.at[ny + j],
            s_cnt.at[j], r_cnt.at[j]))

    xs = pl.ds(pl.multiple_of(x * bx, 128), bx)

    def xcols(i):
        return pl.ds(pl.multiple_of(i * bx, 128), bx)

    top, bottom = pl.ds(0, 16), pl.ds(16, 16)

    def sem(array, it, stage):
        return lambda k: array.at[it, stage, k]

    def gather_first(it):
        send_all("x", lambda i: vb.at[it, 0, y, top, xs], lambda i: vb.at[it, 0, y, top, xcols(i)],
                 sem(s_ag, it, 0), sem(r_ag, it, 0))
        send_all("y", lambda i: vb.at[it, 0, y, bottom, xs], lambda i: vb.at[it, 0, i, bottom, xs],
                 sem(s_ag, it, 1), sem(r_ag, it, 1))

    def forward(it, half, j, place):
        return send_pair(vb.at[(it, 0) + place], vb.at[(it, 1) + place], s_ag.at[it, half, j], r_ag.at[it, half, j])

    def gather_second(it):
        recv_all("x", lambda i: vb.at[it, 0, y, top, xcols(i)], sem(s_ag, it, 0), sem(r_ag, it, 0))
        send_all("y", lambda i: vb.at[it, 0, y, top, :], lambda i: vb.at[it, 0, i, top, :],
                 sem(s_ag, it, 2), sem(r_ag, it, 2))
        recv_all("y", lambda i: vb.at[it, 0, i, bottom, xs], sem(s_ag, it, 1), sem(r_ag, it, 1))
        send_all("x", lambda i: vb.at[it, 0, :, bottom, xs], lambda i: vb.at[it, 0, :, bottom, xcols(i)],
                 sem(s_ag, it, 3), sem(r_ag, it, 3))
        return [forward(it, 4, 0, (y, top)), forward(it, 5, 0, (slice(None), bottom, xs))]

    def gather_third(it, copies):
        for k in near_first(max(nx, ny)):
            if k < ny:
                i = lax.rem(y + ny - k, ny)
                piece = vb.at[it, 0, i, top, :]
                remote(piece, piece, s_ag.at[it, 2, k], r_ag.at[it, 2, k], to_y(i)).wait_recv()
                copies.append(forward(it, 4, k, (i, top)))
            if k < nx:
                i = lax.rem(x + nx - k, nx)
                piece = vb.at[it, 0, :, bottom, xcols(i)]
                remote(piece, piece, s_ag.at[it, 3, k], r_ag.at[it, 3, k], to_x(i)).wait_recv()
                copies.append(forward(it, 5, k, (slice(None), bottom, xcols(i))))
        return copies

    def stack_slot(it, slot):
        def one(j, carry):
            high, low = split2(vb[it, slot, j])
            chunk = slot * ny + j
            vst[it, chunk, 0:32] = high
            vst[it, chunk, 32:64] = low
            vst[it, chunk, 64:96] = high
            return carry
        lax.fori_loop(0, ny, one, 0)

    def extra_slot(slot, ref):
        rows = lax.broadcasted_iota(jnp.int32, (RANK, by), 0)
        for j in range(ny):
            g1, g2, g3 = split3(ref[:, j * by:(j + 1) * by])
            extra = jnp.where(rows < 3, 1.0, jnp.where(rows == 3, g1, jnp.where(rows == 4, g2, jnp.where(rows == 5, g3, 0.0))))
            extra = extra.astype(BF16)
            for it in range(ITERS):
                vst[it, slot * ny + j, 96:128] = extra

    def gram_own(it):
        def one(chunk, acc):
            w = vst[it, chunk]
            return acc + lax.dot_general(w[0:64], w, (((1,), (1,)), ((), ())), preferred_element_type=F32)
        acc = lax.fori_loop(0, ny, one, jnp.zeros((64, 128), F32))
        both = acc[0:32] + acc[32:64]
        gram = both + pltpu.roll(both, 96, 1)
        small = lane[0:8]
        packed = jnp.where(small < 32, gram[0:8], jnp.where(
            small < 64, pltpu.roll(gram[8:16], 32, 1), jnp.where(
                small < 96, pltpu.roll(gram[16:24], 64, 1), pltpu.roll(gram[24:32], 96, 1))))
        gpb[it, 0] = packed
        return send_pair(gpb.at[it, 0], gpb.at[it, 1], s_gp.at[it], r_gp.at[it])

    def gram_send(it, copy):
        copy.wait_recv()
        grb[it, h] = gpb[it, 0] + gpb[it, 1]
        send_all("h", lambda i: grb.at[it, h], lambda i: grb.at[it, i], lambda k: s_gr.at[it, k], lambda k: r_gr.at[it, k])

    def gram_finish(it):
        recv_all("h", lambda i: grb.at[it, i], lambda k: s_gr.at[it, k], lambda k: r_gr.at[it, k])
        total = grb[it, 0]
        for i in range(1, nh):
            total = total + grb[it, i]
        gram = jnp.concatenate([total] + [pltpu.roll(total, 128 - 32 * i, 1) for i in range(1, 4)], axis=0)
        gram = jnp.where(lane < 32, gram, 0.0)
        diagonal = row == lane
        trace = jnp.sum(jnp.sum(jnp.where(diagonal, gram, 0.0), axis=1, keepdims=True), axis=0, keepdims=True)
        hess = gram + jnp.where(diagonal, 0.1 * (trace / RANK), 0.0)

        def pivot(k, a):
            rmask = row == k
            lmask = lane == k
            prow = jnp.sum(jnp.where(rmask, a, 0.0), axis=0, keepdims=True)
            pcol = jnp.sum(jnp.where(lmask, a, 0.0), axis=1, keepdims=True)
            d = jnp.sum(jnp.where(rmask[:, 0:1], pcol, 0.0), axis=0, keepdims=True)
            inv = 1.0 / d
            scaled = jnp.where(lmask[0:1], inv, prow * inv)
            rest = jnp.where(lmask, 0.0, a) - jnp.where(rmask[:, 0:1], 0.0, pcol) * scaled
            return jnp.where(rmask, scaled, rest)
        inverse = lax.fori_loop(0, RANK, pivot, hess)
        return trace, 0.25 * inverse[:, 0:RANK]

    def lhs_of(u):
        first = u.astype(BF16).astype(F32)
        stack = jnp.concatenate([first, first, u - first, offrows], axis=0)
        return stack.T[0:64].astype(BF16)

    def grad_part(it, lhs, store, first, last, acc):
        def one(chunk, acc):
            w = vst[it, chunk]
            eta = jnp.dot(lhs, w, preferred_element_type=F32)
            resid = jnp.exp(eta) - cnt[chunk].astype(F32)
            r1, r2 = split2(resid)
            both = jnp.concatenate([r1, r2], axis=0)
            if store:
                rb[chunk] = both
            return acc + lax.dot_general(w[0:64], both, (((1,), (1,)), ((), ())), preferred_element_type=F32)
        return lax.fori_loop(first, last, one, acc)

    def grad_pack(acc):
        s = acc[0:32] + acc[32:64]
        g = s + pltpu.roll(s, 64, 1)
        return jnp.where(low16, g[0:16], g[16:32])

    zero_acc = jnp.zeros((64, 128), F32)

    def grad_send(n, packed):
        arb[n, h] = packed
        send_all("h", lambda i: arb.at[n, h], lambda i: arb.at[n, i], lambda k: s_ar.at[n, k], lambda k: r_ar.at[n, k])

    def grad_finish(n, u, quarter_inverse):
        recv_all("h", lambda i: arb.at[n, i], lambda k: s_ar.at[n, k], lambda k: r_ar.at[n, k])
        total = arb[n, 0]
        for i in range(1, nh):
            total = total + arb[n, i]
        grad = jnp.concatenate([total, pltpu.roll(total, 64, 1)], axis=0)
        return u - jnp.dot(quarter_inverse, grad, precision=HIGH, preferred_element_type=F32)

    def scatter_start(it, u):
        dup = jnp.where(lane < 64, u, pltpu.roll(u, 64, 1))
        high, low = split2(dup)
        lhs = jnp.concatenate([high, low], axis=0)

        def make(slot):
            def one(j, carry):
                out = jnp.dot(lhs, rb[slot * ny + j], preferred_element_type=F32)
                gp[it, slot, j] = out[0:32] + out[32:64]
                return carry
            lax.fori_loop(0, ny, one, 0)
        make(1)
        first = send_pair(gp.at[it, 1], prs.at[it], s_rs.at[it, 0, 0], r_rs.at[it, 0, 0])
        square = jnp.where(lane < 64, u * u, 0.0)
        square = jnp.sum(jnp.sum(square, axis=1, keepdims=True), axis=0, keepdims=True)
        trb[it, 0, 0] = jnp.broadcast_to(square, (8, 128))
        second = send_pair(trb.at[it, 0, 0], trb.at[it, 0, 1], s_tr.at[it, 0, 0], r_tr.at[it, 0, 0])
        make(0)
        return first, second

    def trace_stage(it, axis, stage, value):
        _, me, _ = axes[axis]
        trb[it, stage, me] = value
        send_all(axis, lambda i: trb.at[it, stage, me], lambda i: trb.at[it, stage, i],
                 sem(s_tr, it, stage), sem(r_tr, it, stage))

    def trace_sum(it, axis, stage):
        _, _, n = axes[axis]
        recv_all(axis, lambda i: trb.at[it, stage, i], sem(s_tr, it, stage), sem(r_tr, it, stage))
        total = trb[it, stage, 0]
        for i in range(1, n):
            total = total + trb[it, stage, i]
        return total

    def scatter_first(it, copies):
        copies[1].wait_recv()
        trace_stage(it, "y", 1, trb[it, 0, 0] + trb[it, 0, 1])
        copies[0].wait_recv()

        def one(j, carry):
            gp[it, 0, j] += prs[it, j]
            return carry
        lax.fori_loop(0, ny, one, 0)
        send_all("y", lambda i: gp.at[it, 0, i, top, :], lambda i: ra1.at[it, i], sem(s_rs, it, 1), sem(r_rs, it, 1))
        send_all("x", lambda i: gp.at[it, 0, :, bottom, xcols(i)], lambda i: rb1.at[it, i], sem(s_rs, it, 2), sem(r_rs, it, 2))
        ra1[it, y] = gp[it, 0, y, 0:16, :]
        rb1[it, x] = gp[it, 0, :, 16:32, xs]

    def scatter_second(it):
        trace_stage(it, "x", 2, trace_sum(it, "y", 1))
        recv_all("y", lambda i: ra1.at[it, i], sem(s_rs, it, 1), sem(r_rs, it, 1))
        total = ra1[it, 0]
        for i in range(1, ny):
            total = total + ra1[it, i]
        a1[it] = total
        send_all("x", lambda i: a1.at[it, :, xcols(i)], lambda i: ra2.at[it, i], sem(s_rs, it, 3), sem(r_rs, it, 3))
        recv_all("x", lambda i: rb1.at[it, i], sem(s_rs, it, 2), sem(r_rs, it, 2))
        total = rb1[it, 0]
        for i in range(1, nx):
            total = total + rb1[it, i]
        b1[it] = total
        send_all("y", lambda i: b1.at[it, i], lambda i: rb2.at[it, i], sem(s_rs, it, 4), sem(r_rs, it, 4))
        ra2[it, x] = a1[it, :, xs]
        rb2[it, y] = b1[it, y]

    def scatter_third(it):
        trace_stage(it, "z", 3, trace_sum(it, "x", 2))
        recv_all("x", lambda i: ra2.at[it, i], sem(s_rs, it, 3), sem(r_rs, it, 3))
        recv_all("y", lambda i: rb2.at[it, i], sem(s_rs, it, 4), sem(r_rs, it, 4))
        total = ra2[it, 0]
        for i in range(1, nx):
            total = total + ra2[it, i]
        rz[it, z, 0:16] = total
        total = rb2[it, 0]
        for i in range(1, ny):
            total = total + rb2[it, i]
        rz[it, z, 16:32] = total
        send_all("z", lambda i: rz.at[it, z], lambda i: rz.at[it, i], sem(s_rs, it, 5), sem(r_rs, it, 5))

    def scatter_finish(it, gram_trace):
        trace_u = trace_sum(it, "z", 3)[0:1, 0:1]
        recv_all("z", lambda i: rz.at[it, i], sem(s_rs, it, 5), sem(r_rs, it, 5))
        total = rz[it, 0]
        for i in range(1, nz):
            total = total + rz[it, i]
        rate = (0.5 * RANK) / trace_u
        level = 0.1 * jnp.sqrt(gram_trace / (RANK * genes) + 1e-06)
        w = vb[it, 0, y, :, xs] - rate * total
        return jnp.where(w > level, w - level, jnp.where(w < -level, w + level, 0.0)) / 1.1

    recv_all("z", lambda i: zbuf.at[i], lambda k: s_z.at[k], lambda k: r_z.at[k])
    for t in range(bx // 128):
        vb[0, 0, y, :, pl.ds(pl.multiple_of(x * bx + t * 128, 128), 128)] = zbuf[2 * t] + zbuf[2 * t + 1]
    gather_first(0)
    pl.semaphore_wait(met_ring, 2)
    for k in range(1, nz):
        signal(met_line, to_z(lax.rem(z + k, nz)))
    for copy in inputs[1:]:
        copy.wait()
    sf = jnp.log(sf_ref[...].astype(F32) / 2000.0)
    sf = jnp.where(core == 0, sf, pltpu.roll(sf, 64, 1))
    o1, o2, o3 = split3(sf)
    offrows = jnp.where(row == 0, o1, jnp.where(row == 1, o2, jnp.where(row == 2, o3, jnp.where(row < 6, 1.0, 0.0))))
    u = jnp.where(core == 0, u_ref[...], pltpu.roll(u_ref[...], 64, 1))
    extra_slot(0, goff_ref)
    pieces = gather_second(0)
    pl.semaphore_wait(met_line, nz - 1)
    sides = sorted({1, nh - 1})
    for k in sides:
        signal(met_far, to_h(lax.rem(h + k, nh)))
    go_copy.wait_recv()
    extra_slot(1, gop)
    lhs = lhs_of(u)
    for copy in local:
        copy.wait()
    pieces = gather_third(0, pieces)
    stack_slot(0, 0)
    gram_copy = gram_own(0)
    acc = grad_part(0, lhs, True, 0, ny, zero_acc)
    pl.semaphore_wait(met_far, len(sides))
    gram_send(0, gram_copy)
    for copy in cnt_copies + pieces:
        copy.wait_recv()
    stack_slot(0, 1)
    acc = grad_part(0, lhs, True, ny, nch, acc)

    for it in range(ITERS):
        if it > 0:
            acc = grad_part(it, lhs_of(u), True, 0, nch, zero_acc)
        grad_send(4 * it, grad_pack(acc))
        copies = scatter_start(it, u)
        gram_trace, quarter_inverse = gram_finish(it)
        scatter_first(it, copies)
        u = grad_finish(4 * it, u, quarter_inverse)
        for turn in range(1, FACTOR_STEPS):
            n = 4 * it + turn
            grad_send(n, grad_pack(grad_part(it, lhs_of(u), False, 0, nch, zero_acc)))
            if turn == 1:
                scatter_second(it)
                scatter_third(it)
            elif turn == 2:
                fresh = scatter_finish(it, gram_trace)
                if it < ITERS - 1:
                    vb[it + 1, 0, y, :, xs] = fresh
                    gather_first(it + 1)
                    pieces = gather_second(it + 1)
                else:
                    vnew[...] = fresh
                    vo_ref[...] = vnew[:, pl.ds(pl.multiple_of((z // 2) * 128, 128), 128)]
            elif it < ITERS - 1:
                pieces = gather_third(it + 1, pieces)
                stack_slot(it + 1, 0)
                gram_copy = gram_own(it + 1)
                for copy in pieces:
                    copy.wait_recv()
                stack_slot(it + 1, 1)
                gram_send(it + 1, gram_copy)
            u = grad_finish(n, u, quarter_inverse)
        if it == ITERS - 1:
            upb[0] = jnp.where(low16, u[0:16], pltpu.roll(u[16:32], 64, 1))
            last = send_pair(upb.at[0], upb.at[1], s_uf.at[0], r_uf.at[0])
            last.wait_recv()
            theirs = upb[1]
            theirs = jnp.concatenate([theirs, pltpu.roll(theirs, 64, 1)], axis=0)
            mine_first = jnp.where(lane < 64, u, pltpu.roll(theirs, 64, 1))
            theirs_first = jnp.where(lane < 64, theirs, pltpu.roll(u, 64, 1))
            uo_ref[...] = jnp.where(core == 0, mine_first, theirs_first)
    for copy in pending:
        copy.wait_send()


def on_device(dims, counts, size_factor, gene_offset, factors, loadings):
    ny, nx, nz, nh = dims
    bx = nz * 64
    by = nx * bx
    slab = ny * by
    nch = 2 * ny
    most = max(ny, nx, nz, nh)
    shard = loadings.reshape(RANK, 64)
    hbm = pl.BlockSpec(memory_space=pltpu.HBM)
    dma = pltpu.SemaphoreType.DMA
    regular = pltpu.SemaphoreType.REGULAR
    vmem = pl.BlockSpec(memory_space=pltpu.VMEM)
    scratch = [
        pltpu.VMEM((1, 128), jnp.int32),
        pltpu.VMEM((1, slab), F32),
        pltpu.VMEM((RANK, 128), F32),
        pltpu.VMEM((RANK, 64), F32),
        pltpu.VMEM((nch, 64, by), jnp.int32),
        pltpu.VMEM((1, slab), F32),
        pltpu.VMEM((nz, RANK, 128), F32),
        pltpu.VMEM((ITERS, 2, ny, RANK, by), F32),
        pltpu.VMEM((ITERS, nch, 128, by), BF16),
        pltpu.VMEM((nch, 128, by), BF16),
        pltpu.VMEM((ITERS, 2, ny, RANK, by), F32),
        pltpu.VMEM((ITERS, ny, RANK, by), F32),
        pltpu.VMEM((ITERS, ny, 16, by), F32),
        pltpu.VMEM((ITERS, nx, ny, 16, bx), F32),
        pltpu.VMEM((ITERS, 16, by), F32),
        pltpu.VMEM((ITERS, ny, 16, bx), F32),
        pltpu.VMEM((ITERS, nx, 16, bx), F32),
        pltpu.VMEM((ITERS, ny, 16, bx), F32),
        pltpu.VMEM((ITERS, nz, RANK, bx), F32),
        pltpu.VMEM((RANK, bx), F32),
        pltpu.VMEM((ITERS, 4, most, 8, 128), F32),
        pltpu.VMEM((ITERS * FACTOR_STEPS, nh, 16, 128), F32),
        pltpu.VMEM((ITERS, nh, 8, 128), F32),
        pltpu.VMEM((ITERS, 2, 8, 128), F32),
        pltpu.VMEM((2, 16, 128), F32),
        dma((4,)), regular, regular, regular, dma((ITERS,)), dma((ITERS,)),
        dma((ny,)), dma((ny,)), dma((ny,)), dma((1,)), dma((1,)),
        dma((nz,)), dma((nz,)),
        dma((ITERS, 6, most)), dma((ITERS, 6, most)),
        dma((ITERS, 6, most)), dma((ITERS, 6, most)),
        dma((ITERS, 4, most)), dma((ITERS, 4, most)),
        dma((ITERS * FACTOR_STEPS, nh)), dma((ITERS * FACTOR_STEPS, nh)),
        dma((ITERS, nh)), dma((ITERS, nh)),
        dma((1,)), dma((1,)),
    ]
    u_next, v_next = pl.pallas_call(
        functools.partial(kernel, dims),
        out_shape=(jax.ShapeDtypeStruct((RANK, 128), F32), jax.ShapeDtypeStruct((RANK, 128), F32)),
        in_specs=[hbm] * 5,
        out_specs=(vmem, vmem),
        scratch_shapes=scratch,
        compiler_params=pltpu.CompilerParams(
            collective_id=0, has_side_effects=True, vmem_limit_bytes=48 * 1024 * 1024),
    )(counts, size_factor.reshape(1, 128), gene_offset.reshape(1, slab), factors, shard)
    odd = lax.rem(lax.axis_index("cell"), 2) == 1
    v_next = jnp.where(odd, v_next[:, 64:], v_next[:, :64])
    return u_next, v_next.reshape(RANK, 1, 64)


def solution(mesh):
    dims = SPLITS[mesh.shape["cell"]] + (mesh.shape["gene"] // 2,)
    return jax.shard_map(
        functools.partial(on_device, dims),
        mesh=mesh,
        in_specs=(
            P("cell", "gene"),
            P("cell"),
            P("gene"),
            P(None, "cell"),
            P(None, "gene", "cell"),
        ),
        out_specs=(P(None, "cell"), P(None, "gene", "cell")),
        check_vma=False,
    )
```

```python
import functools

import jax
import jax.numpy as jnp
from jax import lax
from jax.experimental import pallas as pl
from jax.experimental.pallas import tpu as pltpu
from jax.sharding import PartitionSpec as P

ITERS = 2
FACTOR_STEPS = 4
RANK = 32
MESH = pl.DeviceIdType.MESH
F32 = jnp.float32
BF16 = jnp.bfloat16
HIGH = lax.Precision.HIGHEST
SPLITS = {64: (4, 4, 4), 8: (2, 2, 2)}


def split2(value):
    high = value.astype(BF16)
    return high, (value - high.astype(F32)).astype(BF16)


def split3(value):
    first = value.astype(BF16).astype(F32)
    rest = value - first
    second = rest.astype(BF16).astype(F32)
    return first, second, rest - second


def kernel(dims, cnt_hbm, sf_hbm, goff_hbm, u_hbm, v_hbm, uo_ref, vo_ref,
           sf_ref, goff_ref, u_ref, v_ref, cnt, gop, zbuf, vb, vst, rb, gp, prs, ra1, rb1, a1, b1, ra2, rb2, rz, vnew, trb, arb, grb, gpb, upb,
           s_in, met_ring, met_line, met_far, s_gp, r_gp, s_local, s_cnt, r_cnt, s_go, r_go, s_z, r_z, s_ag, r_ag, s_rs, r_rs, s_tr, r_tr, s_ar, r_ar, s_gr, r_gr,
           s_uf, r_uf):
    ny, nx, nz, nh = dims
    bx = nz * 64
    by = nx * bx
    nch = 2 * ny
    genes = 2 * nh * ny * by
    p = lax.axis_index("cell")
    q = lax.axis_index("gene")
    z = lax.rem(p, nz)
    x = lax.rem(p // nz, nx)
    y = p // (nz * nx)
    core = lax.rem(q, 2)
    h = q // 2

    def to_x(i):
        return {"cell": y * (nx * nz) + i * nz + z, "gene": q}

    def to_y(i):
        return {"cell": i * (nx * nz) + x * nz + z, "gene": q}

    def to_z(i):
        return {"cell": y * (nx * nz) + x * nz + i, "gene": q}

    def to_h(i):
        return {"cell": p, "gene": i * 2 + core}

    pair = {"cell": p, "gene": h * 2 + 1 - core}
    axes = {"x": (to_x, x, nx), "y": (to_y, y, ny), "z": (to_z, z, nz), "h": (to_h, h, nh)}
    pending = []

    def far_first(n):
        return sorted(range(1, n), key=lambda k: -min(k, n - k))

    def near_first(n):
        return sorted(range(1, n), key=lambda k: min(k, n - k))

    def ring(step):
        other = lax.rem(h * nz + z + step + nh * nz, nh * nz)
        return {"cell": y * (nx * nz) + x * nz + lax.rem(other, nz), "gene": (other // nz) * 2 + core}

    def signal(semaphore, device):
        pl.semaphore_signal(semaphore, inc=1, device_id=device, device_id_type=MESH)


    def remote(src, dst, send, recv, device):
        return pltpu.make_async_remote_copy(
            src_ref=src, dst_ref=dst, send_sem=send, recv_sem=recv, device_id=device, device_id_type=MESH)

    def send_all(axis, source, target, send, recv):
        to, me, n = axes[axis]
        for k in far_first(n):
            i = lax.rem(me + k, n)
            copy = remote(source(i), target(me), send(k), recv(k), to(i))
            copy.start()
            pending.append(copy)

    def recv_all(axis, target, send, recv):
        to, me, n = axes[axis]
        for k in range(1, n):
            i = lax.rem(me + n - k, n)
            remote(target(i), target(i), send(k), recv(k), to(i)).wait_recv()

    def send_pair(src, dst, send, recv):
        copy = remote(src, dst, send, recv, pair)
        copy.start()
        pending.append(copy)
        return copy

    lane = lax.broadcasted_iota(jnp.int32, (RANK, 128), 1)
    row = lax.broadcasted_iota(jnp.int32, (RANK, 128), 0)
    low16 = lane[0:16] < 64

    barrier = pltpu.get_barrier_semaphore()
    signal(barrier, pair)
    signal(barrier, ring(1))
    signal(barrier, ring(-1))
    partners = 3
    for axis in ("x", "y", "z"):
        to, me, n = axes[axis]
        for k in range(1, n):
            signal(barrier, to(lax.rem(me + k, n)))
            partners += 1
    inputs = []
    for j, (src, dst) in enumerate(((v_hbm, v_ref), (sf_hbm, sf_ref), (goff_hbm, goff_ref), (u_hbm, u_ref))):
        copy = pltpu.make_async_copy(src, dst, s_in.at[j])
        copy.start()
        inputs.append(copy)
    local = []
    for j in range(ny):
        copy = pltpu.make_async_copy(
            cnt_hbm.at[pl.ds(pl.multiple_of(core * 64, 64), 64), pl.ds(j * by, by)], cnt.at[j], s_local.at[j])
        copy.start()
        local.append(copy)
    inputs[0].wait()
    shard = v_ref[...]
    shard = jnp.concatenate([shard, shard], axis=1)
    zbuf[z] = jnp.where((lane >= 64) == (lax.rem(z, 2) == 1), shard, 0.0)
    pl.semaphore_wait(barrier, partners)

    send_all("z", lambda i: zbuf.at[z], lambda i: zbuf.at[i], lambda k: s_z.at[k], lambda k: r_z.at[k])
    signal(met_ring, ring(1))
    signal(met_ring, ring(-1))
    go_copy = send_pair(goff_hbm, gop, s_go.at[0], r_go.at[0])
    cnt_copies = []
    for j in range(ny):
        cnt_copies.append(send_pair(
            cnt_hbm.at[pl.ds(pl.multiple_of((1 - core) * 64, 64), 64), pl.ds(j * by, by)], cnt.at[ny + j],
            s_cnt.at[j], r_cnt.at[j]))

    xs = pl.ds(pl.multiple_of(x * bx, 128), bx)

    def xcols(i):
        return pl.ds(pl.multiple_of(i * bx, 128), bx)

    top, bottom = pl.ds(0, 16), pl.ds(16, 16)

    def sem(array, it, stage):
        return lambda k: array.at[it, stage, k]

    def gather_first(it):
        send_all("x", lambda i: vb.at[it, 0, y, top, xs], lambda i: vb.at[it, 0, y, top, xcols(i)],
                 sem(s_ag, it, 0), sem(r_ag, it, 0))
        send_all("y", lambda i: vb.at[it, 0, y, bottom, xs], lambda i: vb.at[it, 0, i, bottom, xs],
                 sem(s_ag, it, 1), sem(r_ag, it, 1))

    def forward(it, half, j, place):
        return send_pair(vb.at[(it, 0) + place], vb.at[(it, 1) + place], s_ag.at[it, half, j], r_ag.at[it, half, j])

    def gather_second(it):
        recv_all("x", lambda i: vb.at[it, 0, y, top, xcols(i)], sem(s_ag, it, 0), sem(r_ag, it, 0))
        send_all("y", lambda i: vb.at[it, 0, y, top, :], lambda i: vb.at[it, 0, i, top, :],
                 sem(s_ag, it, 2), sem(r_ag, it, 2))
        recv_all("y", lambda i: vb.at[it, 0, i, bottom, xs], sem(s_ag, it, 1), sem(r_ag, it, 1))
        send_all("x", lambda i: vb.at[it, 0, :, bottom, xs], lambda i: vb.at[it, 0, :, bottom, xcols(i)],
                 sem(s_ag, it, 3), sem(r_ag, it, 3))
        return [forward(it, 4, 0, (y, top)), forward(it, 5, 0, (slice(None), bottom, xs))]

    def gather_third(it, copies):
        for k in near_first(max(nx, ny)):
            if k < ny:
                i = lax.rem(y + ny - k, ny)
                piece = vb.at[it, 0, i, top, :]
                remote(piece, piece, s_ag.at[it, 2, k], r_ag.at[it, 2, k], to_y(i)).wait_recv()
                copies.append(forward(it, 4, k, (i, top)))
            if k < nx:
                i = lax.rem(x + nx - k, nx)
                piece = vb.at[it, 0, :, bottom, xcols(i)]
                remote(piece, piece, s_ag.at[it, 3, k], r_ag.at[it, 3, k], to_x(i)).wait_recv()
                copies.append(forward(it, 5, k, (slice(None), bottom, xcols(i))))
        return copies

    def stack_slot(it, slot):
        def one(j, carry):
            high, low = split2(vb[it, slot, j])
            chunk = slot * ny + j
            vst[it, chunk, 0:32] = high
            vst[it, chunk, 32:64] = low
            vst[it, chunk, 64:96] = high
            return carry
        lax.fori_loop(0, ny, one, 0)

    def extra_slot(slot, ref):
        rows = lax.broadcasted_iota(jnp.int32, (RANK, by), 0)
        for j in range(ny):
            g1, g2, g3 = split3(ref[:, j * by:(j + 1) * by])
            extra = jnp.where(rows < 3, 1.0, jnp.where(rows == 3, g1, jnp.where(rows == 4, g2, jnp.where(rows == 5, g3, 0.0))))
            extra = extra.astype(BF16)
            for it in range(ITERS):
                vst[it, slot * ny + j, 96:128] = extra

    def gram_own(it):
        def one(chunk, acc):
            w = vst[it, chunk]
            return acc + lax.dot_general(w[0:64], w, (((1,), (1,)), ((), ())), preferred_element_type=F32)
        acc = lax.fori_loop(0, ny, one, jnp.zeros((64, 128), F32))
        both = acc[0:32] + acc[32:64]
        gram = both + pltpu.roll(both, 96, 1)
        small = lane[0:8]
        packed = jnp.where(small < 32, gram[0:8], jnp.where(
            small < 64, pltpu.roll(gram[8:16], 32, 1), jnp.where(
                small < 96, pltpu.roll(gram[16:24], 64, 1), pltpu.roll(gram[24:32], 96, 1))))
        gpb[it, 0] = packed
        return send_pair(gpb.at[it, 0], gpb.at[it, 1], s_gp.at[it], r_gp.at[it])

    def gram_send(it, copy):
        copy.wait_recv()
        grb[it, h] = gpb[it, 0] + gpb[it, 1]
        send_all("h", lambda i: grb.at[it, h], lambda i: grb.at[it, i], lambda k: s_gr.at[it, k], lambda k: r_gr.at[it, k])

    def gram_finish(it):
        recv_all("h", lambda i: grb.at[it, i], lambda k: s_gr.at[it, k], lambda k: r_gr.at[it, k])
        total = grb[it, 0]
        for i in range(1, nh):
            total = total + grb[it, i]
        gram = jnp.concatenate([total] + [pltpu.roll(total, 128 - 32 * i, 1) for i in range(1, 4)], axis=0)
        gram = jnp.where(lane < 32, gram, 0.0)
        diagonal = row == lane
        trace = jnp.sum(jnp.sum(jnp.where(diagonal, gram, 0.0), axis=1, keepdims=True), axis=0, keepdims=True)
        hess = gram + jnp.where(diagonal, 0.1 * (trace / RANK), 0.0)

        def pivot(k, a):
            rmask = row == k
            lmask = lane == k
            prow = jnp.sum(jnp.where(rmask, a, 0.0), axis=0, keepdims=True)
            pcol = jnp.sum(jnp.where(lmask, a, 0.0), axis=1, keepdims=True)
            d = jnp.sum(jnp.where(rmask[:, 0:1], pcol, 0.0), axis=0, keepdims=True)
            inv = 1.0 / d
            scaled = jnp.where(lmask[0:1], inv, prow * inv)
            rest = jnp.where(lmask, 0.0, a) - jnp.where(rmask[:, 0:1], 0.0, pcol) * scaled
            return jnp.where(rmask, scaled, rest)
        inverse = lax.fori_loop(0, RANK, pivot, hess)
        return trace, 0.25 * inverse[:, 0:RANK]

    def lhs_of(u):
        first = u.astype(BF16).astype(F32)
        stack = jnp.concatenate([first, first, u - first, offrows], axis=0)
        return stack.T[0:64].astype(BF16)

    def grad_exp(it, lhs, first, last):
        for chunk in range(first, last):
            eta = jnp.dot(lhs, vst[it, chunk], preferred_element_type=F32)
            r1, r2 = split2(jnp.exp(eta) - cnt[chunk].astype(F32))
            rb[chunk] = jnp.concatenate([r1, r2], axis=0)

    def grad_sum(it):
        left = jnp.concatenate([vst[it, chunk, 0:64] for chunk in range(nch)], axis=1)
        right = jnp.concatenate([rb[chunk] for chunk in range(nch)], axis=1)
        return lax.dot_general(left, right, (((1,), (1,)), ((), ())), preferred_element_type=F32)

    def grad_pack(acc):
        s = acc[0:32] + acc[32:64]
        g = s + pltpu.roll(s, 64, 1)
        return jnp.where(low16, g[0:16], g[16:32])

    def grad_send(n, packed):
        arb[n, h] = packed
        send_all("h", lambda i: arb.at[n, h], lambda i: arb.at[n, i], lambda k: s_ar.at[n, k], lambda k: r_ar.at[n, k])

    def grad_finish(n, u, quarter_inverse):
        recv_all("h", lambda i: arb.at[n, i], lambda k: s_ar.at[n, k], lambda k: r_ar.at[n, k])
        total = arb[n, 0]
        for i in range(1, nh):
            total = total + arb[n, i]
        grad = jnp.concatenate([total, pltpu.roll(total, 64, 1)], axis=0)
        return u - jnp.dot(quarter_inverse, grad, precision=HIGH, preferred_element_type=F32)

    def scatter_start(it, u):
        dup = jnp.where(lane < 64, u, pltpu.roll(u, 64, 1))
        high, low = split2(dup)
        lhs = jnp.concatenate([high, low], axis=0)

        def make(slot):
            def one(j, carry):
                out = jnp.dot(lhs, rb[slot * ny + j], preferred_element_type=F32)
                gp[it, slot, j] = out[0:32] + out[32:64]
                return carry
            lax.fori_loop(0, ny, one, 0)
        make(1)
        first = send_pair(gp.at[it, 1], prs.at[it], s_rs.at[it, 0, 0], r_rs.at[it, 0, 0])
        square = jnp.where(lane < 64, u * u, 0.0)
        square = jnp.sum(jnp.sum(square, axis=1, keepdims=True), axis=0, keepdims=True)
        trb[it, 0, 0] = jnp.broadcast_to(square, (8, 128))
        second = send_pair(trb.at[it, 0, 0], trb.at[it, 0, 1], s_tr.at[it, 0, 0], r_tr.at[it, 0, 0])
        make(0)
        return first, second

    def trace_stage(it, axis, stage, value):
        _, me, _ = axes[axis]
        trb[it, stage, me] = value
        send_all(axis, lambda i: trb.at[it, stage, me], lambda i: trb.at[it, stage, i],
                 sem(s_tr, it, stage), sem(r_tr, it, stage))

    def trace_sum(it, axis, stage):
        _, _, n = axes[axis]
        recv_all(axis, lambda i: trb.at[it, stage, i], sem(s_tr, it, stage), sem(r_tr, it, stage))
        total = trb[it, stage, 0]
        for i in range(1, n):
            total = total + trb[it, stage, i]
        return total

    def scatter_first(it, copies):
        copies[1].wait_recv()
        trace_stage(it, "y", 1, trb[it, 0, 0] + trb[it, 0, 1])
        copies[0].wait_recv()

        def one(j, carry):
            gp[it, 0, j] += prs[it, j]
            return carry
        lax.fori_loop(0, ny, one, 0)
        send_all("y", lambda i: gp.at[it, 0, i, top, :], lambda i: ra1.at[it, i], sem(s_rs, it, 1), sem(r_rs, it, 1))
        send_all("x", lambda i: gp.at[it, 0, :, bottom, xcols(i)], lambda i: rb1.at[it, i], sem(s_rs, it, 2), sem(r_rs, it, 2))
        ra1[it, y] = gp[it, 0, y, 0:16, :]
        rb1[it, x] = gp[it, 0, :, 16:32, xs]

    def scatter_second(it):
        trace_stage(it, "x", 2, trace_sum(it, "y", 1))
        recv_all("y", lambda i: ra1.at[it, i], sem(s_rs, it, 1), sem(r_rs, it, 1))
        total = ra1[it, 0]
        for i in range(1, ny):
            total = total + ra1[it, i]
        a1[it] = total
        send_all("x", lambda i: a1.at[it, :, xcols(i)], lambda i: ra2.at[it, i], sem(s_rs, it, 3), sem(r_rs, it, 3))
        recv_all("x", lambda i: rb1.at[it, i], sem(s_rs, it, 2), sem(r_rs, it, 2))
        total = rb1[it, 0]
        for i in range(1, nx):
            total = total + rb1[it, i]
        b1[it] = total
        send_all("y", lambda i: b1.at[it, i], lambda i: rb2.at[it, i], sem(s_rs, it, 4), sem(r_rs, it, 4))
        ra2[it, x] = a1[it, :, xs]
        rb2[it, y] = b1[it, y]

    def scatter_third(it):
        trace_stage(it, "z", 3, trace_sum(it, "x", 2))
        recv_all("x", lambda i: ra2.at[it, i], sem(s_rs, it, 3), sem(r_rs, it, 3))
        recv_all("y", lambda i: rb2.at[it, i], sem(s_rs, it, 4), sem(r_rs, it, 4))
        total = ra2[it, 0]
        for i in range(1, nx):
            total = total + ra2[it, i]
        rz[it, z, 0:16] = total
        total = rb2[it, 0]
        for i in range(1, ny):
            total = total + rb2[it, i]
        rz[it, z, 16:32] = total
        send_all("z", lambda i: rz.at[it, z], lambda i: rz.at[it, i], sem(s_rs, it, 5), sem(r_rs, it, 5))

    def scatter_finish(it, gram_trace):
        trace_u = trace_sum(it, "z", 3)[0:1, 0:1]
        recv_all("z", lambda i: rz.at[it, i], sem(s_rs, it, 5), sem(r_rs, it, 5))
        total = rz[it, 0]
        for i in range(1, nz):
            total = total + rz[it, i]
        rate = (0.5 * RANK) / trace_u
        level = 0.1 * jnp.sqrt(gram_trace / (RANK * genes) + 1e-06)
        w = vb[it, 0, y, :, xs] - rate * total
        return jnp.where(w > level, w - level, jnp.where(w < -level, w + level, 0.0)) / 1.1

    recv_all("z", lambda i: zbuf.at[i], lambda k: s_z.at[k], lambda k: r_z.at[k])
    for t in range(bx // 128):
        vb[0, 0, y, :, pl.ds(pl.multiple_of(x * bx + t * 128, 128), 128)] = zbuf[2 * t] + zbuf[2 * t + 1]
    gather_first(0)
    pl.semaphore_wait(met_ring, 2)
    for k in range(1, nz):
        signal(met_line, to_z(lax.rem(z + k, nz)))
    for copy in inputs[1:]:
        copy.wait()
    sf = jnp.log(sf_ref[...].astype(F32) / 2000.0)
    sf = jnp.where(core == 0, sf, pltpu.roll(sf, 64, 1))
    o1, o2, o3 = split3(sf)
    offrows = jnp.where(row == 0, o1, jnp.where(row == 1, o2, jnp.where(row == 2, o3, jnp.where(row < 6, 1.0, 0.0))))
    u = jnp.where(core == 0, u_ref[...], pltpu.roll(u_ref[...], 64, 1))
    extra_slot(0, goff_ref)
    pieces = gather_second(0)
    pl.semaphore_wait(met_line, nz - 1)
    sides = sorted({1, nh - 1})
    for k in sides:
        signal(met_far, to_h(lax.rem(h + k, nh)))
    go_copy.wait_recv()
    extra_slot(1, gop)
    lhs = lhs_of(u)
    for copy in local:
        copy.wait()
    pieces = gather_third(0, pieces)
    stack_slot(0, 0)
    gram_copy = gram_own(0)
    grad_exp(0, lhs, 0, ny)
    pl.semaphore_wait(met_far, len(sides))
    gram_send(0, gram_copy)
    for copy in cnt_copies + pieces:
        copy.wait_recv()
    stack_slot(0, 1)
    grad_exp(0, lhs, ny, nch)

    for it in range(ITERS):
        if it > 0:
            grad_exp(it, lhs_of(u), 0, nch)
        grad_send(4 * it, grad_pack(grad_sum(it)))
        copies = scatter_start(it, u)
        gram_trace, quarter_inverse = gram_finish(it)
        scatter_first(it, copies)
        u = grad_finish(4 * it, u, quarter_inverse)
        for turn in range(1, FACTOR_STEPS):
            n = 4 * it + turn
            grad_exp(it, lhs_of(u), 0, nch)
            grad_send(n, grad_pack(grad_sum(it)))
            if turn == 1:
                scatter_second(it)
                scatter_third(it)
            elif turn == 2:
                fresh = scatter_finish(it, gram_trace)
                if it < ITERS - 1:
                    vb[it + 1, 0, y, :, xs] = fresh
                    gather_first(it + 1)
                    pieces = gather_second(it + 1)
                else:
                    vnew[...] = fresh
                    vo_ref[...] = vnew[:, pl.ds(pl.multiple_of((z // 2) * 128, 128), 128)]
            elif it < ITERS - 1:
                pieces = gather_third(it + 1, pieces)
                stack_slot(it + 1, 0)
                gram_copy = gram_own(it + 1)
                for copy in pieces:
                    copy.wait_recv()
                stack_slot(it + 1, 1)
                gram_send(it + 1, gram_copy)
            u = grad_finish(n, u, quarter_inverse)
        if it == ITERS - 1:
            upb[0] = jnp.where(low16, u[0:16], pltpu.roll(u[16:32], 64, 1))
            last = send_pair(upb.at[0], upb.at[1], s_uf.at[0], r_uf.at[0])
            last.wait_recv()
            theirs = upb[1]
            theirs = jnp.concatenate([theirs, pltpu.roll(theirs, 64, 1)], axis=0)
            mine_first = jnp.where(lane < 64, u, pltpu.roll(theirs, 64, 1))
            theirs_first = jnp.where(lane < 64, theirs, pltpu.roll(u, 64, 1))
            uo_ref[...] = jnp.where(core == 0, mine_first, theirs_first)
    for copy in pending:
        copy.wait_send()


def on_device(dims, counts, size_factor, gene_offset, factors, loadings):
    ny, nx, nz, nh = dims
    bx = nz * 64
    by = nx * bx
    slab = ny * by
    nch = 2 * ny
    most = max(ny, nx, nz, nh)
    shard = loadings.reshape(RANK, 64)
    hbm = pl.BlockSpec(memory_space=pltpu.HBM)
    dma = pltpu.SemaphoreType.DMA
    regular = pltpu.SemaphoreType.REGULAR
    vmem = pl.BlockSpec(memory_space=pltpu.VMEM)
    scratch = [
        pltpu.VMEM((1, 128), jnp.int32),
        pltpu.VMEM((1, slab), F32),
        pltpu.VMEM((RANK, 128), F32),
        pltpu.VMEM((RANK, 64), F32),
        pltpu.VMEM((nch, 64, by), jnp.int32),
        pltpu.VMEM((1, slab), F32),
        pltpu.VMEM((nz, RANK, 128), F32),
        pltpu.VMEM((ITERS, 2, ny, RANK, by), F32),
        pltpu.VMEM((ITERS, nch, 128, by), BF16),
        pltpu.VMEM((nch, 128, by), BF16),
        pltpu.VMEM((ITERS, 2, ny, RANK, by), F32),
        pltpu.VMEM((ITERS, ny, RANK, by), F32),
        pltpu.VMEM((ITERS, ny, 16, by), F32),
        pltpu.VMEM((ITERS, nx, ny, 16, bx), F32),
        pltpu.VMEM((ITERS, 16, by), F32),
        pltpu.VMEM((ITERS, ny, 16, bx), F32),
        pltpu.VMEM((ITERS, nx, 16, bx), F32),
        pltpu.VMEM((ITERS, ny, 16, bx), F32),
        pltpu.VMEM((ITERS, nz, RANK, bx), F32),
        pltpu.VMEM((RANK, bx), F32),
        pltpu.VMEM((ITERS, 4, most, 8, 128), F32),
        pltpu.VMEM((ITERS * FACTOR_STEPS, nh, 16, 128), F32),
        pltpu.VMEM((ITERS, nh, 8, 128), F32),
        pltpu.VMEM((ITERS, 2, 8, 128), F32),
        pltpu.VMEM((2, 16, 128), F32),
        dma((4,)), regular, regular, regular, dma((ITERS,)), dma((ITERS,)),
        dma((ny,)), dma((ny,)), dma((ny,)), dma((1,)), dma((1,)),
        dma((nz,)), dma((nz,)),
        dma((ITERS, 6, most)), dma((ITERS, 6, most)),
        dma((ITERS, 6, most)), dma((ITERS, 6, most)),
        dma((ITERS, 4, most)), dma((ITERS, 4, most)),
        dma((ITERS * FACTOR_STEPS, nh)), dma((ITERS * FACTOR_STEPS, nh)),
        dma((ITERS, nh)), dma((ITERS, nh)),
        dma((1,)), dma((1,)),
    ]
    u_next, v_next = pl.pallas_call(
        functools.partial(kernel, dims),
        out_shape=(jax.ShapeDtypeStruct((RANK, 128), F32), jax.ShapeDtypeStruct((RANK, 128), F32)),
        in_specs=[hbm] * 5,
        out_specs=(vmem, vmem),
        scratch_shapes=scratch,
        compiler_params=pltpu.CompilerParams(
            collective_id=0, has_side_effects=True, vmem_limit_bytes=64 * 1024 * 1024),
    )(counts, size_factor.reshape(1, 128), gene_offset.reshape(1, slab), factors, shard)
    odd = lax.rem(lax.axis_index("cell"), 2) == 1
    v_next = jnp.where(odd, v_next[:, 64:], v_next[:, :64])
    return u_next, v_next.reshape(RANK, 1, 64)


def solution(mesh):
    dims = SPLITS[mesh.shape["cell"]] + (mesh.shape["gene"] // 2,)
    return jax.shard_map(
        functools.partial(on_device, dims),
        mesh=mesh,
        in_specs=(
            P("cell", "gene"),
            P("cell"),
            P("gene"),
            P(None, "cell"),
            P(None, "gene", "cell"),
        ),
        out_specs=(P(None, "cell"), P(None, "gene", "cell")),
        check_vma=False,
    )
```

```python
import functools

import jax
import jax.numpy as jnp
from jax import lax
from jax.experimental import pallas as pl
from jax.experimental.pallas import tpu as pltpu
from jax.sharding import PartitionSpec as P

ITERS = 2
FACTOR_STEPS = 4
RANK = 32
MESH = pl.DeviceIdType.MESH
PARTS = 2
CELLS = 64 // PARTS
F32 = jnp.float32
BF16 = jnp.bfloat16
HIGH = lax.Precision.HIGHEST
SPLITS = {64: (4, 4, 4), 8: (2, 2, 2)}


def split2(value):
    high = value.astype(BF16)
    return high, (value - high.astype(F32)).astype(BF16)


def split3(value):
    first = value.astype(BF16).astype(F32)
    rest = value - first
    second = rest.astype(BF16).astype(F32)
    return first, second, rest - second


def kernel(dims, cnt_hbm, sf_hbm, goff_hbm, u_hbm, v_hbm, uo_ref, vo_ref,
           sf_ref, goff_ref, u_ref, v_ref, cnt, gop, zbuf, vb, vst, rb, gp, prs, ra1, rb1, a1, b1, ra2, rb2, rz, vnew, trb, arb, grb, gpb, upb,
           s_in, met_ring, met_line, met_far, s_gp, r_gp, s_local, s_cnt, r_cnt, s_go, r_go, s_z, r_z, s_ag, r_ag, s_on, r_on, s_rs, r_rs, s_tr, r_tr, s_ar, r_ar, s_gr, r_gr,
           s_uf, r_uf):
    ny, nx, nz, nh = dims
    bx = nz * 64
    by = nx * bx
    nch = 2 * ny
    genes = 2 * nh * ny * by
    p = lax.axis_index("cell")
    q = lax.axis_index("gene")
    z = lax.rem(p, nz)
    x = lax.rem(p // nz, nx)
    y = p // (nz * nx)
    core = lax.rem(q, 2)
    h = q // 2

    def to_x(i):
        return {"cell": y * (nx * nz) + i * nz + z, "gene": q}

    def to_y(i):
        return {"cell": i * (nx * nz) + x * nz + z, "gene": q}

    def to_z(i):
        return {"cell": y * (nx * nz) + x * nz + i, "gene": q}

    def to_h(i):
        return {"cell": p, "gene": i * 2 + core}

    pair = {"cell": p, "gene": h * 2 + 1 - core}
    axes = {"x": (to_x, x, nx), "y": (to_y, y, ny), "z": (to_z, z, nz), "h": (to_h, h, nh)}
    pending = []

    def far_first(n):
        return sorted(range(1, n), key=lambda k: -min(k, n - k))

    def near_first(n):
        return sorted(range(1, n), key=lambda k: min(k, n - k))

    def ring(step):
        other = lax.rem(h * nz + z + step + nh * nz, nh * nz)
        return {"cell": y * (nx * nz) + x * nz + lax.rem(other, nz), "gene": (other // nz) * 2 + core}

    def signal(semaphore, device):
        pl.semaphore_signal(semaphore, inc=1, device_id=device, device_id_type=MESH)


    def remote(src, dst, send, recv, device):
        return pltpu.make_async_remote_copy(
            src_ref=src, dst_ref=dst, send_sem=send, recv_sem=recv, device_id=device, device_id_type=MESH)

    def send_all(axis, source, target, send, recv):
        to, me, n = axes[axis]
        for k in far_first(n):
            i = lax.rem(me + k, n)
            copy = remote(source(i), target(me), send(k), recv(k), to(i))
            copy.start()
            pending.append(copy)

    def recv_all(axis, target, send, recv):
        to, me, n = axes[axis]
        for k in range(1, n):
            i = lax.rem(me + n - k, n)
            remote(target(i), target(i), send(k), recv(k), to(i)).wait_recv()

    def send_pair(src, dst, send, recv):
        copy = remote(src, dst, send, recv, pair)
        copy.start()
        pending.append(copy)
        return copy

    lane = lax.broadcasted_iota(jnp.int32, (RANK, 128), 1)
    row = lax.broadcasted_iota(jnp.int32, (RANK, 128), 0)

    barrier = pltpu.get_barrier_semaphore()
    signal(barrier, pair)
    signal(barrier, ring(1))
    signal(barrier, ring(-1))
    partners = 3
    for axis in ("x", "y", "z"):
        to, me, n = axes[axis]
        for k in range(1, n):
            signal(barrier, to(lax.rem(me + k, n)))
            partners += 1
    inputs = []
    for j, (src, dst) in enumerate(((v_hbm, v_ref), (sf_hbm, sf_ref), (goff_hbm, goff_ref), (u_hbm, u_ref))):
        copy = pltpu.make_async_copy(src, dst, s_in.at[j])
        copy.start()
        inputs.append(copy)
    local = []
    for j in range(ny):
        copy = pltpu.make_async_copy(
            cnt_hbm.at[pl.ds(pl.multiple_of(core * 64, 64), 64), pl.ds(j * by, by)], cnt.at[j], s_local.at[j])
        copy.start()
        local.append(copy)
    inputs[0].wait()
    shard = v_ref[...]
    shard = jnp.concatenate([shard, shard], axis=1)
    zbuf[z] = jnp.where((lane >= 64) == (lax.rem(z, 2) == 1), shard, 0.0)
    pl.semaphore_wait(barrier, partners)

    send_all("z", lambda i: zbuf.at[z], lambda i: zbuf.at[i], lambda k: s_z.at[k], lambda k: r_z.at[k])
    signal(met_ring, ring(1))
    signal(met_ring, ring(-1))
    go_copy = send_pair(goff_hbm, gop, s_go.at[0], r_go.at[0])
    cnt_copies = []
    for j in range(ny):
        cnt_copies.append(send_pair(
            cnt_hbm.at[pl.ds(pl.multiple_of((1 - core) * 64, 64), 64), pl.ds(j * by, by)], cnt.at[ny + j],
            s_cnt.at[j], r_cnt.at[j]))

    xs = pl.ds(pl.multiple_of(x * bx, 128), bx)

    def xcols(i):
        return pl.ds(pl.multiple_of(i * bx, 128), bx)

    top, bottom = pl.ds(0, 16), pl.ds(16, 16)

    def sem(array, it, stage):
        return lambda k: array.at[it, stage, k]

    def piece(it, half, iy, ix):
        return vb.at[it, 0, iy, top if half == 0 else bottom, xcols(ix)]

    def onward(it, half, j):
        if half == 0:
            iy, ix = y, lax.rem(x + nx - j, nx)
        else:
            iy, ix = lax.rem(y + ny - j, ny), x
        send_all("yx"[half], lambda i: piece(it, half, iy, ix), lambda i: piece(it, half, iy, ix),
                 lambda k: s_on.at[it, half, k, j], lambda k: r_on.at[it, half, k, j])

    def gather_first(it):
        send_all("x", lambda i: piece(it, 0, y, x), lambda i: piece(it, 0, y, i), sem(s_ag, it, 0), sem(r_ag, it, 0))
        send_all("y", lambda i: piece(it, 1, y, x), lambda i: piece(it, 1, i, x), sem(s_ag, it, 1), sem(r_ag, it, 1))
        onward(it, 0, 0)
        onward(it, 1, 0)

    def forward(it, half, j, place):
        return send_pair(vb.at[(it, 0) + place], vb.at[(it, 1) + place], s_ag.at[it, half, j], r_ag.at[it, half, j])

    def arrived(it, half, k):
        if half == 0:
            here = piece(it, 0, y, lax.rem(x + nx - k, nx))
            remote(here, here, s_ag.at[it, 0, k], r_ag.at[it, 0, k], to_x(lax.rem(x + nx - k, nx))).wait_recv()
        else:
            here = piece(it, 1, lax.rem(y + ny - k, ny), x)
            remote(here, here, s_ag.at[it, 1, k], r_ag.at[it, 1, k], to_y(lax.rem(y + ny - k, ny))).wait_recv()

    def gather_second(it):
        for k in near_first(max(nx, ny)):
            if k < nx:
                arrived(it, 0, k)
                onward(it, 0, k)
            if k < ny:
                arrived(it, 1, k)
                onward(it, 1, k)
        return [forward(it, 4, 0, (y, top)), forward(it, 5, 0, (slice(None), bottom, xs))]

    def gather_third(it, copies):
        for k in near_first(max(nx, ny)):
            if k < ny:
                i = lax.rem(y + ny - k, ny)
                for j in range(nx):
                    here = piece(it, 0, i, lax.rem(x + nx - j, nx))
                    remote(here, here, s_on.at[it, 0, k, j], r_on.at[it, 0, k, j], to_y(i)).wait_recv()
                copies.append(forward(it, 4, k, (i, top)))
            if k < nx:
                i = lax.rem(x + nx - k, nx)
                for j in range(ny):
                    here = piece(it, 1, lax.rem(y + ny - j, ny), i)
                    remote(here, here, s_on.at[it, 1, k, j], r_on.at[it, 1, k, j], to_x(i)).wait_recv()
                copies.append(forward(it, 5, k, (slice(None), bottom, xcols(i))))
        return copies

    def stack_slot(it, slot):
        def one(j, carry):
            high, low = split2(vb[it, slot, j])
            chunk = slot * ny + j
            vst[it, chunk, 0:32] = high
            vst[it, chunk, 32:64] = low
            vst[it, chunk, 64:96] = high
            return carry
        lax.fori_loop(0, ny, one, 0)

    def extra_slot(slot, ref):
        rows = lax.broadcasted_iota(jnp.int32, (RANK, by), 0)
        for j in range(ny):
            g1, g2, g3 = split3(ref[:, j * by:(j + 1) * by])
            extra = jnp.where(rows < 3, 1.0, jnp.where(rows == 3, g1, jnp.where(rows == 4, g2, jnp.where(rows == 5, g3, 0.0))))
            extra = extra.astype(BF16)
            for it in range(ITERS):
                vst[it, slot * ny + j, 96:128] = extra

    def gram_own(it):
        def one(chunk, acc):
            w = vst[it, chunk]
            return acc + lax.dot_general(w[0:64], w, (((1,), (1,)), ((), ())), preferred_element_type=F32)
        acc = lax.fori_loop(0, ny, one, jnp.zeros((64, 128), F32))
        both = acc[0:32] + acc[32:64]
        gram = both + pltpu.roll(both, 96, 1)
        small = lane[0:8]
        packed = jnp.where(small < 32, gram[0:8], jnp.where(
            small < 64, pltpu.roll(gram[8:16], 32, 1), jnp.where(
                small < 96, pltpu.roll(gram[16:24], 64, 1), pltpu.roll(gram[24:32], 96, 1))))
        gpb[it, 0] = packed
        return send_pair(gpb.at[it, 0], gpb.at[it, 1], s_gp.at[it], r_gp.at[it])

    def gram_send(it, copy):
        copy.wait_recv()
        grb[it, h] = gpb[it, 0] + gpb[it, 1]
        send_all("h", lambda i: grb.at[it, h], lambda i: grb.at[it, i], lambda k: s_gr.at[it, k], lambda k: r_gr.at[it, k])

    def gram_finish(it):
        recv_all("h", lambda i: grb.at[it, i], lambda k: s_gr.at[it, k], lambda k: r_gr.at[it, k])
        total = grb[it, 0]
        for i in range(1, nh):
            total = total + grb[it, i]
        gram = jnp.concatenate([total] + [pltpu.roll(total, 128 - 32 * i, 1) for i in range(1, 4)], axis=0)
        gram = jnp.where(lane < 32, gram, 0.0)
        diagonal = row == lane
        trace = jnp.sum(jnp.sum(jnp.where(diagonal, gram, 0.0), axis=1, keepdims=True), axis=0, keepdims=True)
        hess = gram + jnp.where(diagonal, 0.1 * (trace / RANK), 0.0)

        inverse = hess
        for base in range(0, RANK, 8):
            columns = [jnp.broadcast_to(inverse[:, base + j:base + j + 1], (RANK, 128)) for j in range(8)]
            for i in range(8):
                k = base + i
                column, rmask, lmask = columns[i], row == k, lane == k
                inv = 1.0 / column[k:k + 1]
                scaled = jnp.where(lmask[0:1], inv, inverse[k:k + 1] * inv)
                inverse = jnp.where(rmask, scaled, jnp.where(lmask, 0.0, inverse) - column * scaled)
                for j in range(i + 1, 8):
                    entry = columns[j][k:k + 1] * inv
                    columns[j] = jnp.where(rmask, entry, columns[j] - column * entry)
        quarter = 0.25 * jnp.where(lane < 32, inverse, 0.0)
        wide = quarter + pltpu.roll(quarter, 32, 1) + pltpu.roll(quarter, 64, 1)
        return trace, split2(jnp.concatenate([wide] * 4, axis=0))

    third = (lax.broadcasted_iota(jnp.int32, (CELLS, 128), 1) // 32) == 2
    rows8 = CELLS // 4
    lanes8 = lax.broadcasted_iota(jnp.int32, (rows8, 128), 1) // 32

    def grad_exp(it, part, u, first, last):
        high = u.astype(BF16).astype(F32)
        lhs = jnp.where(third, u - high, high).astype(BF16)
        for chunk in range(first, last):
            eta = jnp.dot(lhs, vst[it, chunk], preferred_element_type=F32)
            r1, r2 = split2(jnp.exp(eta) - cnt[chunk, part * CELLS:(part + 1) * CELLS].astype(F32))
            rb[chunk, 2 * part * CELLS:2 * (part + 1) * CELLS] = jnp.concatenate([r1, r2], axis=0)

    def grad_sum(it, part):
        left = jnp.concatenate([rb[chunk, 2 * part * CELLS:2 * (part + 1) * CELLS] for chunk in range(nch)], axis=1)
        right = jnp.concatenate([vst[it, chunk, 0:64] for chunk in range(nch)], axis=1)
        out = lax.dot_general(left, right, (((1,), (1,)), ((), ())), preferred_element_type=F32)
        half = out[0:CELLS] + out[CELLS:2 * CELLS]
        twice = jnp.concatenate([half, half], axis=1)
        g = twice + pltpu.roll(twice, 96, 1)
        quarters = [g[i * rows8:(i + 1) * rows8] for i in range(4)]
        return jnp.where(lanes8 == 0, quarters[0], jnp.where(lanes8 == 1, quarters[1], jnp.where(
            lanes8 == 2, quarters[2], quarters[3])))

    def grad_send(n, part, packed):
        arb[n, part, h] = packed
        send_all("h", lambda i: arb.at[n, part, h], lambda i: arb.at[n, part, i],
                 lambda k: s_ar.at[n, part, k], lambda k: r_ar.at[n, part, k])

    def grad_finish(n, part, u, weights):
        recv_all("h", lambda i: arb.at[n, part, i], lambda k: s_ar.at[n, part, k], lambda k: r_ar.at[n, part, k])
        total = arb[n, part, 0]
        for i in range(1, nh):
            total = total + arb[n, part, i]
        spread = jnp.concatenate([jnp.where(lanes8 == i, total, 0.0) for i in range(4)], axis=0)
        high, low = split2(spread)
        step = jnp.dot(high, weights[0], preferred_element_type=F32)
        step += jnp.dot(low, weights[0], preferred_element_type=F32)
        step += jnp.dot(high, weights[1], preferred_element_type=F32)
        return u - step

    def scatter_start(it, u):
        rows = [x for part in u for x in (part, part)]
        high, low = split2(jnp.concatenate(rows, axis=0).T[0:32])
        lhs = jnp.concatenate([high, low], axis=0)

        def make(slot, j):
            out = jnp.dot(lhs, rb[slot * ny + j], preferred_element_type=F32)
            gp[it, slot, j] = out[0:32] + out[32:64]

        first = []
        for j in range(ny):
            make(1, j)
            first.append(send_pair(gp.at[it, 1, j], prs.at[it, j], s_rs.at[it, 0, j], r_rs.at[it, 0, j]))
        whole = jnp.concatenate(u, axis=0)
        square = jnp.where(lax.broadcasted_iota(jnp.int32, (64, 128), 1) < 32, whole * whole, 0.0)
        square = jnp.sum(jnp.sum(square, axis=1, keepdims=True), axis=0, keepdims=True)
        trb[it, 0, 0] = jnp.broadcast_to(square, (8, 128))
        second = send_pair(trb.at[it, 0, 0], trb.at[it, 0, 1], s_tr.at[it, 0, 0], r_tr.at[it, 0, 0])
        for j in range(ny):
            make(0, j)
        return first, second

    def trace_stage(it, axis, stage, value):
        _, me, _ = axes[axis]
        trb[it, stage, me] = value
        send_all(axis, lambda i: trb.at[it, stage, me], lambda i: trb.at[it, stage, i],
                 sem(s_tr, it, stage), sem(r_tr, it, stage))

    def trace_sum(it, axis, stage):
        _, _, n = axes[axis]
        recv_all(axis, lambda i: trb.at[it, stage, i], sem(s_tr, it, stage), sem(r_tr, it, stage))
        total = trb[it, stage, 0]
        for i in range(1, n):
            total = total + trb[it, stage, i]
        return total

    def scatter_first(it, copies):
        copies[1].wait_recv()
        trace_stage(it, "y", 1, trb[it, 0, 0] + trb[it, 0, 1])
        for j, copy in enumerate(copies[0]):
            copy.wait_recv()
            gp[it, 0, j] += prs[it, j]
        send_all("y", lambda i: gp.at[it, 0, i, top, :], lambda i: ra1.at[it, i], sem(s_rs, it, 1), sem(r_rs, it, 1))
        send_all("x", lambda i: gp.at[it, 0, :, bottom, xcols(i)], lambda i: rb1.at[it, i], sem(s_rs, it, 2), sem(r_rs, it, 2))
        ra1[it, y] = gp[it, 0, y, 0:16, :]
        rb1[it, x] = gp[it, 0, :, 16:32, xs]

    def scatter_second(it):
        trace_stage(it, "x", 2, trace_sum(it, "y", 1))
        recv_all("y", lambda i: ra1.at[it, i], sem(s_rs, it, 1), sem(r_rs, it, 1))
        total = ra1[it, 0]
        for i in range(1, ny):
            total = total + ra1[it, i]
        a1[it] = total
        send_all("x", lambda i: a1.at[it, :, xcols(i)], lambda i: ra2.at[it, i], sem(s_rs, it, 3), sem(r_rs, it, 3))
        recv_all("x", lambda i: rb1.at[it, i], sem(s_rs, it, 2), sem(r_rs, it, 2))
        total = rb1[it, 0]
        for i in range(1, nx):
            total = total + rb1[it, i]
        b1[it] = total
        send_all("y", lambda i: b1.at[it, i], lambda i: rb2.at[it, i], sem(s_rs, it, 4), sem(r_rs, it, 4))
        ra2[it, x] = a1[it, :, xs]
        rb2[it, y] = b1[it, y]

    def scatter_third(it):
        trace_stage(it, "z", 3, trace_sum(it, "x", 2))
        recv_all("x", lambda i: ra2.at[it, i], sem(s_rs, it, 3), sem(r_rs, it, 3))
        recv_all("y", lambda i: rb2.at[it, i], sem(s_rs, it, 4), sem(r_rs, it, 4))
        total = ra2[it, 0]
        for i in range(1, nx):
            total = total + ra2[it, i]
        rz[it, z, 0:16] = total
        total = rb2[it, 0]
        for i in range(1, ny):
            total = total + rb2[it, i]
        rz[it, z, 16:32] = total
        send_all("z", lambda i: rz.at[it, z], lambda i: rz.at[it, i], sem(s_rs, it, 5), sem(r_rs, it, 5))

    def scatter_finish(it, gram_trace):
        trace_u = trace_sum(it, "z", 3)[0:1, 0:1]
        recv_all("z", lambda i: rz.at[it, i], sem(s_rs, it, 5), sem(r_rs, it, 5))
        total = rz[it, 0]
        for i in range(1, nz):
            total = total + rz[it, i]
        rate = (0.5 * RANK) / trace_u
        level = 0.1 * jnp.sqrt(gram_trace / (RANK * genes) + 1e-06)
        w = vb[it, 0, y, :, xs] - rate * total
        return jnp.where(w > level, w - level, jnp.where(w < -level, w + level, 0.0)) / 1.1

    recv_all("z", lambda i: zbuf.at[i], lambda k: s_z.at[k], lambda k: r_z.at[k])
    for t in range(bx // 128):
        vb[0, 0, y, :, pl.ds(pl.multiple_of(x * bx + t * 128, 128), 128)] = zbuf[2 * t] + zbuf[2 * t + 1]
    gather_first(0)
    pl.semaphore_wait(met_ring, 2)
    for k in range(1, nz):
        signal(met_line, to_z(lax.rem(z + k, nz)))
    for copy in inputs[1:]:
        copy.wait()
    sf = jnp.log(sf_ref[...].astype(F32) / 2000.0)
    sf = jnp.where(core == 0, sf, pltpu.roll(sf, 64, 1))
    o1, o2, o3 = split3(sf)
    offrows = jnp.where(row == 0, o1, jnp.where(row == 1, o2, jnp.where(row == 2, o3, jnp.where(row < 6, 1.0, 0.0))))
    u = jnp.where(core == 0, u_ref[...], pltpu.roll(u_ref[...], 64, 1))
    u = jnp.concatenate([u, u, u, offrows], axis=0).T
    u = [u[part * CELLS:(part + 1) * CELLS] for part in range(PARTS)]
    extra_slot(0, goff_ref)
    pieces = gather_second(0)
    pl.semaphore_wait(met_line, nz - 1)
    sides = sorted({1, nh - 1})
    for k in sides:
        signal(met_far, to_h(lax.rem(h + k, nh)))
    go_copy.wait_recv()
    extra_slot(1, gop)
    for copy in local:
        copy.wait()
    pieces = gather_third(0, pieces)
    stack_slot(0, 0)
    gram_copy = gram_own(0)
    for part in range(PARTS):
        grad_exp(0, part, u[part], 0, ny)
        if part == 0:
            pl.semaphore_wait(met_far, len(sides))
            gram_send(0, gram_copy)
    for copy in cnt_copies + pieces:
        copy.wait_recv()
    stack_slot(0, 1)

    weights = None
    for it in range(ITERS):
        for turn in range(FACTOR_STEPS):
            n = 4 * it + turn
            for part in range(PARTS):
                if n > 0:
                    u[part] = grad_finish(n - 1, part, u[part], weights)
                grad_exp(it, part, u[part], ny if n == 0 else 0, nch)
                grad_send(n, part, grad_sum(it, part))
            if turn == 0:
                copies = scatter_start(it, u)
                scatter_first(it, copies)
                gram_trace, weights = gram_finish(it)
            elif turn == 1:
                scatter_second(it)
                scatter_third(it)
            elif turn == 2:
                fresh = scatter_finish(it, gram_trace)
                if it < ITERS - 1:
                    vb[it + 1, 0, y, :, xs] = fresh
                    gather_first(it + 1)
                    pieces = gather_second(it + 1)
                else:
                    vnew[...] = fresh
                    vo_ref[...] = vnew[:, pl.ds(pl.multiple_of((z // 2) * 128, 128), 128)]
            elif it < ITERS - 1:
                pieces = gather_third(it + 1, pieces)
                stack_slot(it + 1, 0)
                gram_copy = gram_own(it + 1)
                for copy in pieces:
                    copy.wait_recv()
                stack_slot(it + 1, 1)
                gram_send(it + 1, gram_copy)
    copies = []
    for part in range(PARTS):
        u[part] = grad_finish(ITERS * FACTOR_STEPS - 1, part, u[part], weights)
        upb[0, part] = u[part]
        copies.append(send_pair(upb.at[0, part], upb.at[1, part], s_uf.at[part], r_uf.at[part]))
    for copy in copies:
        copy.wait_recv()
    theirs = [upb[1, part] for part in range(PARTS)]
    mine_first = jnp.concatenate(u + theirs, axis=0)
    theirs_first = jnp.concatenate(theirs + u, axis=0)
    uo_ref[...] = jnp.where(core == 0, mine_first, theirs_first).T[0:32]
    for copy in pending:
        copy.wait_send()


def on_device(dims, counts, size_factor, gene_offset, factors, loadings):
    ny, nx, nz, nh = dims
    bx = nz * 64
    by = nx * bx
    slab = ny * by
    nch = 2 * ny
    most = max(ny, nx, nz, nh)
    shard = loadings.reshape(RANK, 64)
    hbm = pl.BlockSpec(memory_space=pltpu.HBM)
    dma = pltpu.SemaphoreType.DMA
    regular = pltpu.SemaphoreType.REGULAR
    vmem = pl.BlockSpec(memory_space=pltpu.VMEM)
    scratch = [
        pltpu.VMEM((1, 128), jnp.int32),
        pltpu.VMEM((1, slab), F32),
        pltpu.VMEM((RANK, 128), F32),
        pltpu.VMEM((RANK, 64), F32),
        pltpu.VMEM((nch, 64, by), jnp.int32),
        pltpu.VMEM((1, slab), F32),
        pltpu.VMEM((nz, RANK, 128), F32),
        pltpu.VMEM((ITERS, 2, ny, RANK, by), F32),
        pltpu.VMEM((ITERS, nch, 128, by), BF16),
        pltpu.VMEM((nch, 128, by), BF16),
        pltpu.VMEM((ITERS, 2, ny, RANK, by), F32),
        pltpu.VMEM((ITERS, ny, RANK, by), F32),
        pltpu.VMEM((ITERS, ny, 16, by), F32),
        pltpu.VMEM((ITERS, nx, ny, 16, bx), F32),
        pltpu.VMEM((ITERS, 16, by), F32),
        pltpu.VMEM((ITERS, ny, 16, bx), F32),
        pltpu.VMEM((ITERS, nx, 16, bx), F32),
        pltpu.VMEM((ITERS, ny, 16, bx), F32),
        pltpu.VMEM((ITERS, nz, RANK, bx), F32),
        pltpu.VMEM((RANK, bx), F32),
        pltpu.VMEM((ITERS, 4, most, 8, 128), F32),
        pltpu.VMEM((ITERS * FACTOR_STEPS, PARTS, nh, CELLS // 4, 128), F32),
        pltpu.VMEM((ITERS, nh, 8, 128), F32),
        pltpu.VMEM((ITERS, 2, 8, 128), F32),
        pltpu.VMEM((2, PARTS, CELLS, 128), F32),
        dma((4,)), regular, regular, regular, dma((ITERS,)), dma((ITERS,)),
        dma((ny,)), dma((ny,)), dma((ny,)), dma((1,)), dma((1,)),
        dma((nz,)), dma((nz,)),
        dma((ITERS, 6, most)), dma((ITERS, 6, most)),
        dma((ITERS, 2, most, most)), dma((ITERS, 2, most, most)),
        dma((ITERS, 6, most)), dma((ITERS, 6, most)),
        dma((ITERS, 4, most)), dma((ITERS, 4, most)),
        dma((ITERS * FACTOR_STEPS, PARTS, nh)), dma((ITERS * FACTOR_STEPS, PARTS, nh)),
        dma((ITERS, nh)), dma((ITERS, nh)),
        dma((PARTS,)), dma((PARTS,)),
    ]
    u_next, v_next = pl.pallas_call(
        functools.partial(kernel, dims),
        out_shape=(jax.ShapeDtypeStruct((RANK, 128), F32), jax.ShapeDtypeStruct((RANK, 128), F32)),
        in_specs=[hbm] * 5,
        out_specs=(vmem, vmem),
        scratch_shapes=scratch,
        compiler_params=pltpu.CompilerParams(
            collective_id=0, has_side_effects=True, vmem_limit_bytes=64 * 1024 * 1024),
    )(counts, size_factor.reshape(1, 128), gene_offset.reshape(1, slab), factors, shard)
    odd = lax.rem(lax.axis_index("cell"), 2) == 1
    v_next = jnp.where(odd, v_next[:, 64:], v_next[:, :64])
    return u_next, v_next.reshape(RANK, 1, 64)


def solution(mesh):
    dims = SPLITS[mesh.shape["cell"]] + (mesh.shape["gene"] // 2,)
    return jax.shard_map(
        functools.partial(on_device, dims),
        mesh=mesh,
        in_specs=(
            P("cell", "gene"),
            P("cell"),
            P("gene"),
            P(None, "cell"),
            P(None, "gene", "cell"),
        ),
        out_specs=(P(None, "cell"), P(None, "gene", "cell")),
        check_vma=False,
    )
```

```python
import functools

import jax
import jax.numpy as jnp
from jax import lax
from jax.experimental import pallas as pl
from jax.experimental.pallas import tpu as pltpu
from jax.sharding import PartitionSpec as P

ITERS = 2
FACTOR_STEPS = 4
RANK = 32
MESH = pl.DeviceIdType.MESH
PARTS = 2
CELLS = 64 // PARTS
F32 = jnp.float32
BF16 = jnp.bfloat16
HIGH = lax.Precision.HIGHEST
SPLITS = {64: (4, 4, 4), 8: (2, 2, 2)}


def split2(value):
    high = value.astype(BF16)
    return high, (value - high.astype(F32)).astype(BF16)


def split3(value):
    first = value.astype(BF16).astype(F32)
    rest = value - first
    second = rest.astype(BF16).astype(F32)
    return first, second, rest - second


def kernel(dims, cnt_hbm, sf_hbm, goff_hbm, u_hbm, v_hbm, uo_ref, vo_ref,
           sf_ref, goff_ref, u_ref, v_ref, cnt, gop, zbuf, vb, vst, rb, gp, prs, ra1, rb1, a1, b1, ra2, rb2, rz, vnew, arb, grb, gpb, upb,
           s_in, met_ring, met_line, met_far, s_gp, r_gp, s_local, s_cnt, r_cnt, s_go, r_go, s_z, r_z, s_ag, r_ag, s_rs, r_rs, s_ar, r_ar, s_gr, r_gr,
           s_uf, r_uf):
    ny, nx, nz, nh = dims
    bx = nz * 64
    by = nx * bx
    nch = 2 * ny
    genes = 2 * nh * ny * by
    p = lax.axis_index("cell")
    q = lax.axis_index("gene")
    z = p & (nz - 1)
    x = (p // nz) & (nx - 1)
    y = p // (nz * nx)
    core = q & 1
    h = q // 2

    def to_x(i):
        return {"cell": y * (nx * nz) + i * nz + z, "gene": q}

    def to_y(i):
        return {"cell": i * (nx * nz) + x * nz + z, "gene": q}

    def to_z(i):
        return {"cell": y * (nx * nz) + x * nz + i, "gene": q}

    def to_h(i):
        return {"cell": p, "gene": i * 2 + core}

    pair = {"cell": p, "gene": h * 2 + 1 - core}
    axes = {"x": (to_x, x, nx), "y": (to_y, y, ny), "z": (to_z, z, nz), "h": (to_h, h, nh)}
    places = {axis: [(me + k) & (n - 1) for k in range(n)] for axis, (_, me, n) in axes.items()}
    devices = {axis: [axes[axis][0](i) for i in places[axis]] for axis in axes}
    pending = []

    def far_first(n):
        return sorted(range(1, n), key=lambda k: -min(k, n - k))

    def near_first(n):
        return sorted(range(1, n), key=lambda k: min(k, n - k))

    def ring(step):
        other = lax.rem(h * nz + z + step + nh * nz, nh * nz)
        return {"cell": y * (nx * nz) + x * nz + lax.rem(other, nz), "gene": (other // nz) * 2 + core}

    def signal(semaphore, device):
        pl.semaphore_signal(semaphore, inc=1, device_id=device, device_id_type=MESH)


    def remote(src, dst, send, recv, device):
        return pltpu.make_async_remote_copy(
            src_ref=src, dst_ref=dst, send_sem=send, recv_sem=recv, device_id=device, device_id_type=MESH)

    def send_all(axis, source, target, send, recv):
        to, me, n = axes[axis]
        for k in far_first(n):
            copy = remote(source(places[axis][k]), target(me), send(k), recv(k), devices[axis][k])
            copy.start()
            pending.append(copy)

    def recv_all(axis, target, send, recv):
        to, me, n = axes[axis]
        for k in range(1, n):
            here = target(places[axis][n - k])
            remote(here, here, send(k), recv(k), devices[axis][n - k]).wait_recv()

    def send_pair(src, dst, send, recv):
        copy = remote(src, dst, send, recv, pair)
        copy.start()
        pending.append(copy)
        return copy

    lane = lax.broadcasted_iota(jnp.int32, (RANK, 128), 1)
    row = lax.broadcasted_iota(jnp.int32, (RANK, 128), 0)

    barrier = pltpu.get_barrier_semaphore()
    signal(barrier, pair)
    signal(barrier, ring(1))
    signal(barrier, ring(-1))
    partners = 3
    for axis in ("x", "y", "z"):
        to, me, n = axes[axis]
        for k in range(1, n):
            signal(barrier, to(lax.rem(me + k, n)))
            partners += 1
    inputs = []
    for j, (src, dst) in enumerate(((v_hbm, v_ref), (sf_hbm, sf_ref), (goff_hbm, goff_ref), (u_hbm, u_ref))):
        copy = pltpu.make_async_copy(src, dst, s_in.at[j])
        copy.start()
        inputs.append(copy)
    local = []
    for j in range(ny):
        copy = pltpu.make_async_copy(
            cnt_hbm.at[pl.ds(pl.multiple_of(core * 64, 64), 64), pl.ds(j * by, by)], cnt.at[j], s_local.at[j])
        copy.start()
        local.append(copy)
    inputs[0].wait()
    shard = v_ref[...]
    shard = jnp.concatenate([shard, shard], axis=1)
    zbuf[z] = jnp.where((lane >= 64) == (lax.rem(z, 2) == 1), shard, 0.0)
    pl.semaphore_wait(barrier, partners)

    send_all("z", lambda i: zbuf.at[z], lambda i: zbuf.at[i], lambda k: s_z.at[k], lambda k: r_z.at[k])
    signal(met_ring, ring(1))
    signal(met_ring, ring(-1))
    go_copy = send_pair(goff_hbm, gop, s_go.at[0], r_go.at[0])
    cnt_copies = []
    for j in range(ny):
        cnt_copies.append(send_pair(
            cnt_hbm.at[pl.ds(pl.multiple_of((1 - core) * 64, 64), 64), pl.ds(j * by, by)], cnt.at[ny + j],
            s_cnt.at[j], r_cnt.at[j]))

    xs = pl.ds(pl.multiple_of(x * bx, 128), bx)

    def xcols(i):
        return pl.ds(pl.multiple_of(i * bx, 128), bx)

    top, bottom = pl.ds(0, 16), pl.ds(16, 16)

    def sem(array, it, stage):
        return lambda k: array.at[it, stage, k]

    def gather_first(it):
        send_all("x", lambda i: vb.at[it, 0, y, top, xs], lambda i: vb.at[it, 0, y, top, xcols(i)],
                 sem(s_ag, it, 0), sem(r_ag, it, 0))
        send_all("y", lambda i: vb.at[it, 0, y, bottom, xs], lambda i: vb.at[it, 0, i, bottom, xs],
                 sem(s_ag, it, 1), sem(r_ag, it, 1))

    def forward(it, half, j, place):
        return send_pair(vb.at[(it, 0) + place], vb.at[(it, 1) + place], s_ag.at[it, half, j], r_ag.at[it, half, j])

    def gather_second(it):
        recv_all("x", lambda i: vb.at[it, 0, y, top, xcols(i)], sem(s_ag, it, 0), sem(r_ag, it, 0))
        send_all("y", lambda i: vb.at[it, 0, y, top, :], lambda i: vb.at[it, 0, i, top, :],
                 sem(s_ag, it, 2), sem(r_ag, it, 2))
        recv_all("y", lambda i: vb.at[it, 0, i, bottom, xs], sem(s_ag, it, 1), sem(r_ag, it, 1))
        send_all("x", lambda i: vb.at[it, 0, :, bottom, xs], lambda i: vb.at[it, 0, :, bottom, xcols(i)],
                 sem(s_ag, it, 3), sem(r_ag, it, 3))
        return [forward(it, 4, 0, (y, top)), forward(it, 5, 0, (slice(None), bottom, xs))]

    def gather_third(it, copies):
        for k in near_first(max(nx, ny)):
            if k < ny:
                i = lax.rem(y + ny - k, ny)
                piece = vb.at[it, 0, i, top, :]
                remote(piece, piece, s_ag.at[it, 2, k], r_ag.at[it, 2, k], to_y(i)).wait_recv()
                copies.append(forward(it, 4, k, (i, top)))
            if k < nx:
                i = lax.rem(x + nx - k, nx)
                piece = vb.at[it, 0, :, bottom, xcols(i)]
                remote(piece, piece, s_ag.at[it, 3, k], r_ag.at[it, 3, k], to_x(i)).wait_recv()
                copies.append(forward(it, 5, k, (slice(None), bottom, xcols(i))))
        return copies

    def stack_slot(it, slot):
        def one(j, carry):
            high, low = split2(vb[it, slot, j])
            chunk = slot * ny + j
            vst[it, chunk, 0:32] = high
            vst[it, chunk, 32:64] = low
            vst[it, chunk, 64:96] = high
            return carry
        lax.fori_loop(0, ny, one, 0)

    def extra_slot(slot, ref):
        rows = lax.broadcasted_iota(jnp.int32, (RANK, by), 0)
        for j in range(ny):
            g1, g2, g3 = split3(ref[:, j * by:(j + 1) * by])
            extra = jnp.where(rows < 3, 1.0, jnp.where(rows == 3, g1, jnp.where(rows == 4, g2, jnp.where(rows == 5, g3, 0.0))))
            extra = extra.astype(BF16)
            for it in range(ITERS):
                vst[it, slot * ny + j, 96:128] = extra

    def gram_own(it):
        def one(chunk, acc):
            w = vst[it, chunk]
            return acc + lax.dot_general(w[0:64], w, (((1,), (1,)), ((), ())), preferred_element_type=F32)
        acc = lax.fori_loop(0, ny, one, jnp.zeros((64, 128), F32))
        both = acc[0:32] + acc[32:64]
        gram = both + pltpu.roll(both, 96, 1)
        small = lane[0:8]
        packed = jnp.where(small < 32, gram[0:8], jnp.where(
            small < 64, pltpu.roll(gram[8:16], 32, 1), jnp.where(
                small < 96, pltpu.roll(gram[16:24], 64, 1), pltpu.roll(gram[24:32], 96, 1))))
        gpb[it, 0] = packed
        return send_pair(gpb.at[it, 0], gpb.at[it, 1], s_gp.at[it], r_gp.at[it])

    def gram_send(it, copy):
        copy.wait_recv()
        grb[it, h] = gpb[it, 0] + gpb[it, 1]
        send_all("h", lambda i: grb.at[it, h], lambda i: grb.at[it, i], lambda k: s_gr.at[it, k], lambda k: r_gr.at[it, k])

    def gram_finish(it):
        recv_all("h", lambda i: grb.at[it, i], lambda k: s_gr.at[it, k], lambda k: r_gr.at[it, k])
        total = grb[it, 0]
        for i in range(1, nh):
            total = total + grb[it, i]
        gram = jnp.concatenate([total] + [pltpu.roll(total, 128 - 32 * i, 1) for i in range(1, 4)], axis=0)
        gram = jnp.where(lane < 32, gram, 0.0)
        diagonal = row == lane
        trace = jnp.sum(jnp.sum(jnp.where(diagonal, gram, 0.0), axis=1, keepdims=True), axis=0, keepdims=True)
        hess = gram + jnp.where(diagonal, 0.1 * (trace / RANK), 0.0)

        inverse = hess
        for base in range(0, RANK, 8):
            columns = [jnp.broadcast_to(inverse[:, base + j:base + j + 1], (RANK, 128)) for j in range(8)]
            for i in range(8):
                k = base + i
                column, rmask, lmask = columns[i], row == k, lane == k
                inv = 1.0 / column[k:k + 1]
                scaled = jnp.where(lmask[0:1], inv, inverse[k:k + 1] * inv)
                inverse = jnp.where(rmask, scaled, jnp.where(lmask, 0.0, inverse) - column * scaled)
                for j in range(i + 1, 8):
                    entry = columns[j][k:k + 1] * inv
                    columns[j] = jnp.where(rmask, entry, columns[j] - column * entry)
        quarter = 0.25 * jnp.where(lane < 32, inverse, 0.0)
        wide = quarter + pltpu.roll(quarter, 32, 1) + pltpu.roll(quarter, 64, 1)
        return trace, split2(jnp.concatenate([wide] * 4, axis=0))

    third = (lax.broadcasted_iota(jnp.int32, (CELLS, 128), 1) // 32) == 2
    rows8 = CELLS // 4
    lanes8 = lax.broadcasted_iota(jnp.int32, (rows8, 128), 1) // 32

    def grad_exp(it, part, u, first, last):
        high = u.astype(BF16).astype(F32)
        lhs = jnp.where(third, u - high, high).astype(BF16)
        for chunk in range(first, last):
            eta = jnp.dot(lhs, vst[it, chunk], preferred_element_type=F32)
            r1, r2 = split2(jnp.exp(eta) - cnt[chunk, part * CELLS:(part + 1) * CELLS].astype(F32))
            rb[chunk, 2 * part * CELLS:2 * (part + 1) * CELLS] = jnp.concatenate([r1, r2], axis=0)

    def grad_sum(it, part):
        left = jnp.concatenate([rb[chunk, 2 * part * CELLS:2 * (part + 1) * CELLS] for chunk in range(nch)], axis=1)
        right = jnp.concatenate([vst[it, chunk, 0:64] for chunk in range(nch)], axis=1)
        out = lax.dot_general(left, right, (((1,), (1,)), ((), ())), preferred_element_type=F32)
        half = out[0:CELLS] + out[CELLS:2 * CELLS]
        twice = jnp.concatenate([half, half], axis=1)
        g = twice + pltpu.roll(twice, 96, 1)
        quarters = [g[i * rows8:(i + 1) * rows8] for i in range(4)]
        return jnp.where(lanes8 == 0, quarters[0], jnp.where(lanes8 == 1, quarters[1], jnp.where(
            lanes8 == 2, quarters[2], quarters[3])))

    def grad_send(n, part, packed):
        arb[n, part, h] = packed
        send_all("h", lambda i: arb.at[n, part, h], lambda i: arb.at[n, part, i],
                 lambda k: s_ar.at[n, part, k], lambda k: r_ar.at[n, part, k])

    def grad_finish(n, part, u, weights):
        recv_all("h", lambda i: arb.at[n, part, i], lambda k: s_ar.at[n, part, k], lambda k: r_ar.at[n, part, k])
        total = arb[n, part, 0]
        for i in range(1, nh):
            total = total + arb[n, part, i]
        spread = jnp.concatenate([jnp.where(lanes8 == i, total, 0.0) for i in range(4)], axis=0)
        high, low = split2(spread)
        step = jnp.dot(high, weights[0], preferred_element_type=F32)
        step += jnp.dot(low, weights[0], preferred_element_type=F32)
        step += jnp.dot(high, weights[1], preferred_element_type=F32)
        return u - step

    def scatter_start(it, u):
        rows = [x for part in u for x in (part, part)]
        high, low = split2(jnp.concatenate(rows, axis=0).T[0:32])
        lhs = jnp.concatenate([high, low], axis=0)

        whole = jnp.concatenate(u, axis=0)
        square = jnp.where(lax.broadcasted_iota(jnp.int32, (64, 128), 1) < 32, whole * whole, 0.0)
        square = jnp.sum(jnp.sum(square, axis=1, keepdims=True), axis=0, keepdims=True)
        square = jnp.broadcast_to(square, (8, by))

        def make(slot, j):
            out = jnp.dot(lhs, rb[slot * ny + j], preferred_element_type=F32)
            gp[it, slot, j, 0:32] = out[0:32] + out[32:64]
            gp[it, slot, j, 32:40] = square

        copies = []
        for j in range(ny):
            make(1, j)
            copies.append(send_pair(gp.at[it, 1, j], prs.at[it, j], s_rs.at[it, 0, j], r_rs.at[it, 0, j]))
        for j in range(ny):
            make(0, j)
        return copies

    def scatter_first(it, copies):
        for j, copy in enumerate(copies):
            copy.wait_recv()
            gp[it, 0, j] += prs[it, j]
        send_all("y", lambda i: gp.at[it, 0, i, top, :], lambda i: ra1.at[it, i], sem(s_rs, it, 1), sem(r_rs, it, 1))
        send_all("x", lambda i: gp.at[it, 0, :, pl.ds(16, 24), xcols(i)], lambda i: rb1.at[it, i], sem(s_rs, it, 2), sem(r_rs, it, 2))
        ra1[it, y] = gp[it, 0, y, 0:16, :]
        rb1[it, x] = gp[it, 0, :, 16:40, xs]

    def scatter_second(it):
        recv_all("y", lambda i: ra1.at[it, i], sem(s_rs, it, 1), sem(r_rs, it, 1))
        total = ra1[it, 0]
        for i in range(1, ny):
            total = total + ra1[it, i]
        a1[it] = total
        send_all("x", lambda i: a1.at[it, :, xcols(i)], lambda i: ra2.at[it, i], sem(s_rs, it, 3), sem(r_rs, it, 3))
        recv_all("x", lambda i: rb1.at[it, i], sem(s_rs, it, 2), sem(r_rs, it, 2))
        total = rb1[it, 0]
        for i in range(1, nx):
            total = total + rb1[it, i]
        b1[it] = total
        send_all("y", lambda i: b1.at[it, i], lambda i: rb2.at[it, i], sem(s_rs, it, 4), sem(r_rs, it, 4))
        ra2[it, x] = a1[it, :, xs]
        rb2[it, y] = b1[it, y]

    def scatter_third(it):
        recv_all("x", lambda i: ra2.at[it, i], sem(s_rs, it, 3), sem(r_rs, it, 3))
        recv_all("y", lambda i: rb2.at[it, i], sem(s_rs, it, 4), sem(r_rs, it, 4))
        total = ra2[it, 0]
        for i in range(1, nx):
            total = total + ra2[it, i]
        rz[it, z, 0:16] = total
        total = rb2[it, 0]
        for i in range(1, ny):
            total = total + rb2[it, i]
        rz[it, z, 16:40] = total
        send_all("z", lambda i: rz.at[it, z], lambda i: rz.at[it, i], sem(s_rs, it, 5), sem(r_rs, it, 5))

    def scatter_finish(it, gram_trace):
        recv_all("z", lambda i: rz.at[it, i], sem(s_rs, it, 5), sem(r_rs, it, 5))
        total = rz[it, 0]
        for i in range(1, nz):
            total = total + rz[it, i]
        rate = (0.5 * RANK) / total[32:33, 0:1]
        level = 0.1 * jnp.sqrt(gram_trace / (RANK * genes) + 1e-06)
        w = vb[it, 0, y, :, xs] - rate * total[0:32]
        return jnp.where(w > level, w - level, jnp.where(w < -level, w + level, 0.0)) / 1.1

    recv_all("z", lambda i: zbuf.at[i], lambda k: s_z.at[k], lambda k: r_z.at[k])
    for t in range(bx // 128):
        vb[0, 0, y, :, pl.ds(pl.multiple_of(x * bx + t * 128, 128), 128)] = zbuf[2 * t] + zbuf[2 * t + 1]
    gather_first(0)
    pl.semaphore_wait(met_ring, 2)
    for k in range(1, nz):
        signal(met_line, to_z(lax.rem(z + k, nz)))
    for copy in inputs[1:]:
        copy.wait()
    sf = jnp.log(sf_ref[...].astype(F32) / 2000.0)
    sf = jnp.where(core == 0, sf, pltpu.roll(sf, 64, 1))
    o1, o2, o3 = split3(sf)
    offrows = jnp.where(row == 0, o1, jnp.where(row == 1, o2, jnp.where(row == 2, o3, jnp.where(row < 6, 1.0, 0.0))))
    u = jnp.where(core == 0, u_ref[...], pltpu.roll(u_ref[...], 64, 1))
    u = jnp.concatenate([u, u, u, offrows], axis=0).T
    u = [u[part * CELLS:(part + 1) * CELLS] for part in range(PARTS)]
    extra_slot(0, goff_ref)
    pieces = gather_second(0)
    pl.semaphore_wait(met_line, nz - 1)
    sides = sorted({1, nh - 1})
    for k in sides:
        signal(met_far, to_h(lax.rem(h + k, nh)))
    go_copy.wait_recv()
    extra_slot(1, gop)
    for copy in local:
        copy.wait()
    pieces = gather_third(0, pieces)
    stack_slot(0, 0)
    gram_copy = gram_own(0)
    for part in range(PARTS):
        grad_exp(0, part, u[part], 0, ny)
        if part == 0:
            pl.semaphore_wait(met_far, len(sides))
            gram_send(0, gram_copy)
    for copy in cnt_copies + pieces:
        copy.wait_recv()
    stack_slot(0, 1)

    weights = None
    for it in range(ITERS):
        for turn in range(FACTOR_STEPS):
            n = 4 * it + turn
            for part in range(PARTS):
                if n > 0:
                    u[part] = grad_finish(n - 1, part, u[part], weights)
                grad_exp(it, part, u[part], ny if n == 0 else 0, nch)
                grad_send(n, part, grad_sum(it, part))
            if turn == 0:
                copies = scatter_start(it, u)
                scatter_first(it, copies)
                gram_trace, weights = gram_finish(it)
            elif turn == 1:
                scatter_second(it)
                scatter_third(it)
            elif turn == 2:
                fresh = scatter_finish(it, gram_trace)
                if it < ITERS - 1:
                    vb[it + 1, 0, y, :, xs] = fresh
                    gather_first(it + 1)
                    pieces = gather_second(it + 1)
                else:
                    vnew[...] = fresh
                    vo_ref[...] = vnew[:, pl.ds(pl.multiple_of((z // 2) * 128, 128), 128)]
            elif it < ITERS - 1:
                pieces = gather_third(it + 1, pieces)
                stack_slot(it + 1, 0)
                gram_copy = gram_own(it + 1)
                for copy in pieces:
                    copy.wait_recv()
                stack_slot(it + 1, 1)
                gram_send(it + 1, gram_copy)
    copies = []
    for part in range(PARTS):
        u[part] = grad_finish(ITERS * FACTOR_STEPS - 1, part, u[part], weights)
        upb[0, part] = u[part]
        copies.append(send_pair(upb.at[0, part], upb.at[1, part], s_uf.at[part], r_uf.at[part]))
    for copy in copies:
        copy.wait_recv()
    theirs = [upb[1, part] for part in range(PARTS)]
    mine_first = jnp.concatenate(u + theirs, axis=0)
    theirs_first = jnp.concatenate(theirs + u, axis=0)
    uo_ref[...] = jnp.where(core == 0, mine_first, theirs_first).T[0:32]
    for copy in pending:
        copy.wait_send()


def on_device(dims, counts, size_factor, gene_offset, factors, loadings):
    ny, nx, nz, nh = dims
    bx = nz * 64
    by = nx * bx
    slab = ny * by
    nch = 2 * ny
    most = max(ny, nx, nz, nh)
    shard = loadings.reshape(RANK, 64)
    hbm = pl.BlockSpec(memory_space=pltpu.HBM)
    dma = pltpu.SemaphoreType.DMA
    regular = pltpu.SemaphoreType.REGULAR
    vmem = pl.BlockSpec(memory_space=pltpu.VMEM)
    scratch = [
        pltpu.VMEM((1, 128), jnp.int32),
        pltpu.VMEM((1, slab), F32),
        pltpu.VMEM((RANK, 128), F32),
        pltpu.VMEM((RANK, 64), F32),
        pltpu.VMEM((nch, 64, by), jnp.int32),
        pltpu.VMEM((1, slab), F32),
        pltpu.VMEM((nz, RANK, 128), F32),
        pltpu.VMEM((ITERS, 2, ny, RANK, by), F32),
        pltpu.VMEM((ITERS, nch, 128, by), BF16),
        pltpu.VMEM((nch, 128, by), BF16),
        pltpu.VMEM((ITERS, 2, ny, RANK + 8, by), F32),
        pltpu.VMEM((ITERS, ny, RANK + 8, by), F32),
        pltpu.VMEM((ITERS, ny, 16, by), F32),
        pltpu.VMEM((ITERS, nx, ny, 24, bx), F32),
        pltpu.VMEM((ITERS, 16, by), F32),
        pltpu.VMEM((ITERS, ny, 24, bx), F32),
        pltpu.VMEM((ITERS, nx, 16, bx), F32),
        pltpu.VMEM((ITERS, ny, 24, bx), F32),
        pltpu.VMEM((ITERS, nz, RANK + 8, bx), F32),
        pltpu.VMEM((RANK, bx), F32),
        pltpu.VMEM((ITERS * FACTOR_STEPS, PARTS, nh, CELLS // 4, 128), F32),
        pltpu.VMEM((ITERS, nh, 8, 128), F32),
        pltpu.VMEM((ITERS, 2, 8, 128), F32),
        pltpu.VMEM((2, PARTS, CELLS, 128), F32),
        dma((4,)), regular, regular, regular, dma((ITERS,)), dma((ITERS,)),
        dma((ny,)), dma((ny,)), dma((ny,)), dma((1,)), dma((1,)),
        dma((nz,)), dma((nz,)),
        dma((ITERS, 6, most)), dma((ITERS, 6, most)),
        dma((ITERS, 6, most)), dma((ITERS, 6, most)),
        dma((ITERS * FACTOR_STEPS, PARTS, nh)), dma((ITERS * FACTOR_STEPS, PARTS, nh)),
        dma((ITERS, nh)), dma((ITERS, nh)),
        dma((PARTS,)), dma((PARTS,)),
    ]
    u_next, v_next = pl.pallas_call(
        functools.partial(kernel, dims),
        out_shape=(jax.ShapeDtypeStruct((RANK, 128), F32), jax.ShapeDtypeStruct((RANK, 128), F32)),
        in_specs=[hbm] * 5,
        out_specs=(vmem, vmem),
        scratch_shapes=scratch,
        compiler_params=pltpu.CompilerParams(
            collective_id=0, has_side_effects=True, vmem_limit_bytes=48 * 1024 * 1024),
    )(*[pltpu.with_memory_space_constraint(v, pltpu.HBM) for v in (counts, size_factor.reshape(1, 128), gene_offset.reshape(1, slab), factors, shard)])
    odd = lax.rem(lax.axis_index("cell"), 2) == 1
    v_next = jnp.where(odd, v_next[:, 64:], v_next[:, :64])
    return u_next, v_next.reshape(RANK, 1, 64)


def solution(mesh):
    dims = SPLITS[mesh.shape["cell"]] + (mesh.shape["gene"] // 2,)
    return jax.shard_map(
        functools.partial(on_device, dims),
        mesh=mesh,
        in_specs=(
            P("cell", "gene"),
            P("cell"),
            P("gene"),
            P(None, "cell"),
            P(None, "gene", "cell"),
        ),
        out_specs=(P(None, "cell"), P(None, "gene", "cell")),
        check_vma=False,
    )
```

```python
import functools

import jax
import jax.numpy as jnp
from jax import lax
from jax.experimental import pallas as pl
from jax.experimental.pallas import tpu as pltpu
from jax.sharding import PartitionSpec as P

ITERS = 2
FACTOR_STEPS = 4
RANK = 32
MESH = pl.DeviceIdType.MESH
PARTS = 2
CELLS = 64 // PARTS
F32 = jnp.float32
BF16 = jnp.bfloat16
HIGH = lax.Precision.HIGHEST
SPLITS = {64: (4, 4, 4), 8: (2, 2, 2)}


def split2(value):
    high = value.astype(BF16)
    return high, (value - high.astype(F32)).astype(BF16)


def split3(value):
    first = value.astype(BF16).astype(F32)
    rest = value - first
    second = rest.astype(BF16).astype(F32)
    return first, second, rest - second


def kernel(dims, cnt_hbm, sf_hbm, goff_hbm, u_hbm, v_hbm, uo_ref, vo_ref,
           sf_ref, goff_ref, u_ref, v_ref, cnt, gop, zbuf, vb, vst, rb, gp, prs, ra1, rb1, a1, b1, ra2, rb2, rz, vnew, arb, grb, gpb, upb,
           s_in, met_ring, met_line, met_far, s_gp, r_gp, s_local, s_cnt, r_cnt, s_go, r_go, s_z, r_z, s_ag, r_ag, s_rs, r_rs, s_ar, r_ar, s_gr, r_gr,
           s_uf, r_uf):
    ny, nx, nz, nh = dims
    bx = nz * 64
    by = nx * bx
    nch = 2 * ny
    genes = 2 * nh * ny * by
    p = lax.axis_index("cell")
    q = lax.axis_index("gene")
    z = p & (nz - 1)
    x = (p // nz) & (nx - 1)
    y = p // (nz * nx)
    core = q & 1
    h = q // 2

    def to_x(i):
        return {"cell": y * (nx * nz) + i * nz + z, "gene": q}

    def to_y(i):
        return {"cell": i * (nx * nz) + x * nz + z, "gene": q}

    def to_z(i):
        return {"cell": y * (nx * nz) + x * nz + i, "gene": q}

    def to_h(i):
        return {"cell": p, "gene": i * 2 + core}

    pair = {"cell": p, "gene": h * 2 + 1 - core}
    axes = {"x": (to_x, x, nx), "y": (to_y, y, ny), "z": (to_z, z, nz), "h": (to_h, h, nh)}
    places = {axis: [(me + k) & (n - 1) for k in range(n)] for axis, (_, me, n) in axes.items()}
    devices = {axis: [axes[axis][0](i) for i in places[axis]] for axis in axes}
    pending = []

    def far_first(n):
        return sorted(range(1, n), key=lambda k: -min(k, n - k))

    def near_first(n):
        return sorted(range(1, n), key=lambda k: min(k, n - k))

    def ring(step):
        other = lax.rem(h * nz + z + step + nh * nz, nh * nz)
        return {"cell": y * (nx * nz) + x * nz + lax.rem(other, nz), "gene": (other // nz) * 2 + core}

    def signal(semaphore, device):
        pl.semaphore_signal(semaphore, inc=1, device_id=device, device_id_type=MESH)


    def remote(src, dst, send, recv, device):
        return pltpu.make_async_remote_copy(
            src_ref=src, dst_ref=dst, send_sem=send, recv_sem=recv, device_id=device, device_id_type=MESH)

    def send_all(axis, source, target, send, recv):
        to, me, n = axes[axis]
        for k in far_first(n):
            copy = remote(source(places[axis][k]), target(me), send(k), recv(k), devices[axis][k])
            copy.start()
            pending.append(copy)

    def recv_all(axis, target, send, recv):
        to, me, n = axes[axis]
        for k in range(1, n):
            here = target(places[axis][n - k])
            remote(here, here, send(k), recv(k), devices[axis][n - k]).wait_recv()

    def send_pair(src, dst, send, recv):
        copy = remote(src, dst, send, recv, pair)
        copy.start()
        pending.append(copy)
        return copy

    lane = lax.broadcasted_iota(jnp.int32, (RANK, 128), 1)
    row = lax.broadcasted_iota(jnp.int32, (RANK, 128), 0)

    barrier = pltpu.get_barrier_semaphore()
    signal(barrier, pair)
    signal(barrier, ring(1))
    signal(barrier, ring(-1))
    partners = 3
    for axis in ("x", "y", "z"):
        to, me, n = axes[axis]
        for k in range(1, n):
            signal(barrier, to(lax.rem(me + k, n)))
            partners += 1
    inputs = []
    for j, (src, dst) in enumerate(((v_hbm, v_ref), (sf_hbm, sf_ref), (goff_hbm, goff_ref), (u_hbm, u_ref))):
        copy = pltpu.make_async_copy(src, dst, s_in.at[j])
        copy.start()
        inputs.append(copy)
    local = []
    for j in range(ny):
        copy = pltpu.make_async_copy(
            cnt_hbm.at[pl.ds(pl.multiple_of(core * 64, 64), 64), pl.ds(j * by, by)], cnt.at[j], s_local.at[j])
        copy.start()
        local.append(copy)
    inputs[0].wait()
    shard = v_ref[...]
    shard = jnp.concatenate([shard, shard], axis=1)
    zbuf[z] = jnp.where((lane >= 64) == (lax.rem(z, 2) == 1), shard, 0.0)
    pl.semaphore_wait(barrier, partners)

    send_all("z", lambda i: zbuf.at[z], lambda i: zbuf.at[i], lambda k: s_z.at[k], lambda k: r_z.at[k])
    signal(met_ring, ring(1))
    signal(met_ring, ring(-1))
    go_copy = send_pair(goff_hbm, gop, s_go.at[0], r_go.at[0])
    cnt_copies = []
    for j in range(ny):
        cnt_copies.append(send_pair(
            cnt_hbm.at[pl.ds(pl.multiple_of((1 - core) * 64, 64), 64), pl.ds(j * by, by)], cnt.at[ny + j],
            s_cnt.at[j], r_cnt.at[j]))

    xs = pl.ds(pl.multiple_of(x * bx, 128), bx)

    def xcols(i):
        return pl.ds(pl.multiple_of(i * bx, 128), bx)

    top, bottom = pl.ds(0, 16), pl.ds(16, 16)

    def sem(array, it, stage):
        return lambda k: array.at[it, stage, k]

    def gather_first(it):
        send_all("x", lambda i: vb.at[it, 0, y, top, xs], lambda i: vb.at[it, 0, y, top, xcols(i)],
                 sem(s_ag, it, 0), sem(r_ag, it, 0))
        send_all("y", lambda i: vb.at[it, 0, y, bottom, xs], lambda i: vb.at[it, 0, i, bottom, xs],
                 sem(s_ag, it, 1), sem(r_ag, it, 1))

    def forward(it, half, j, place):
        return send_pair(vb.at[(it, 0) + place], vb.at[(it, 1) + place], s_ag.at[it, half, j], r_ag.at[it, half, j])

    def gather_second(it):
        recv_all("x", lambda i: vb.at[it, 0, y, top, xcols(i)], sem(s_ag, it, 0), sem(r_ag, it, 0))
        send_all("y", lambda i: vb.at[it, 0, y, top, :], lambda i: vb.at[it, 0, i, top, :],
                 sem(s_ag, it, 2), sem(r_ag, it, 2))
        recv_all("y", lambda i: vb.at[it, 0, i, bottom, xs], sem(s_ag, it, 1), sem(r_ag, it, 1))
        send_all("x", lambda i: vb.at[it, 0, :, bottom, xs], lambda i: vb.at[it, 0, :, bottom, xcols(i)],
                 sem(s_ag, it, 3), sem(r_ag, it, 3))
        return [forward(it, 4, 0, (y, top)), forward(it, 5, 0, (slice(None), bottom, xs))]

    def gather_third(it, copies):
        for k in near_first(max(nx, ny)):
            if k < ny:
                i = lax.rem(y + ny - k, ny)
                piece = vb.at[it, 0, i, top, :]
                remote(piece, piece, s_ag.at[it, 2, k], r_ag.at[it, 2, k], to_y(i)).wait_recv()
                copies.append(forward(it, 4, k, (i, top)))
            if k < nx:
                i = lax.rem(x + nx - k, nx)
                piece = vb.at[it, 0, :, bottom, xcols(i)]
                remote(piece, piece, s_ag.at[it, 3, k], r_ag.at[it, 3, k], to_x(i)).wait_recv()
                copies.append(forward(it, 5, k, (slice(None), bottom, xcols(i))))
        return copies

    def stack_slot(it, slot):
        for j in range(ny):
            high, low = split2(vb[it, slot, j])
            chunk = slot * ny + j
            vst[it, chunk, 0:32] = high
            vst[it, chunk, 32:64] = low
            vst[it, chunk, 64:96] = high

    def extra_slot(slot, ref):
        rows = lax.broadcasted_iota(jnp.int32, (RANK, by), 0)
        for j in range(ny):
            g1, g2, g3 = split3(ref[:, j * by:(j + 1) * by])
            extra = jnp.where(rows < 3, 1.0, jnp.where(rows == 3, g1, jnp.where(rows == 4, g2, jnp.where(rows == 5, g3, 0.0))))
            extra = extra.astype(BF16)
            for it in range(ITERS):
                vst[it, slot * ny + j, 96:128] = extra

    def gram_own(it):
        left = jnp.concatenate([vst[it, chunk, 0:64] for chunk in range(ny)], axis=1)
        right = jnp.concatenate([vst[it, chunk] for chunk in range(ny)], axis=1)
        acc = lax.dot_general(left, right, (((1,), (1,)), ((), ())), preferred_element_type=F32)
        both = acc[0:32] + acc[32:64]
        gram = both + pltpu.roll(both, 96, 1)
        small = lane[0:8]
        packed = jnp.where(small < 32, gram[0:8], jnp.where(
            small < 64, pltpu.roll(gram[8:16], 32, 1), jnp.where(
                small < 96, pltpu.roll(gram[16:24], 64, 1), pltpu.roll(gram[24:32], 96, 1))))
        gpb[it, 0] = packed
        return send_pair(gpb.at[it, 0], gpb.at[it, 1], s_gp.at[it], r_gp.at[it])

    def gram_send(it, copy):
        copy.wait_recv()
        grb[it, h] = gpb[it, 0] + gpb[it, 1]
        send_all("h", lambda i: grb.at[it, h], lambda i: grb.at[it, i], lambda k: s_gr.at[it, k], lambda k: r_gr.at[it, k])

    def gram_finish(it):
        recv_all("h", lambda i: grb.at[it, i], lambda k: s_gr.at[it, k], lambda k: r_gr.at[it, k])
        total = grb[it, 0]
        for i in range(1, nh):
            total = total + grb[it, i]
        gram = jnp.concatenate([total] + [pltpu.roll(total, 128 - 32 * i, 1) for i in range(1, 4)], axis=0)
        gram = jnp.where(lane < 32, gram, 0.0)
        diagonal = row == lane
        trace = jnp.sum(jnp.sum(jnp.where(diagonal, gram, 0.0), axis=1, keepdims=True), axis=0, keepdims=True)
        hess = gram + jnp.where(diagonal, 0.1 * (trace / RANK), 0.0)

        inverse = hess
        for base in range(0, RANK, 8):
            columns = [jnp.broadcast_to(inverse[:, base + j:base + j + 1], (RANK, 128)) for j in range(8)]
            for i in range(8):
                k = base + i
                column, rmask, lmask = columns[i], row == k, lane == k
                inv = 1.0 / column[k:k + 1]
                scaled = jnp.where(lmask[0:1], inv, inverse[k:k + 1] * inv)
                inverse = jnp.where(rmask, scaled, jnp.where(lmask, 0.0, inverse) - column * scaled)
                for j in range(i + 1, 8):
                    entry = columns[j][k:k + 1] * inv
                    columns[j] = jnp.where(rmask, entry, columns[j] - column * entry)
        quarter = 0.25 * jnp.where(lane < 32, inverse, 0.0)
        wide = quarter + pltpu.roll(quarter, 32, 1) + pltpu.roll(quarter, 64, 1)
        high, low = split2(jnp.concatenate([wide] * 4, axis=0))
        return trace, jnp.concatenate([high, high, low], axis=0)

    third = (lax.broadcasted_iota(jnp.int32, (CELLS, 128), 1) // 32) == 2
    rows8 = CELLS // 4
    lanes8 = lax.broadcasted_iota(jnp.int32, (rows8, 128), 1) // 32

    def grad_exp(it, part, u, first, last):
        high = u.astype(BF16).astype(F32)
        lhs = jnp.where(third, u - high, high).astype(BF16)
        for chunk in range(first, last):
            eta = jnp.dot(lhs, vst[it, chunk], preferred_element_type=F32)
            r1, r2 = split2(jnp.exp(eta) - cnt[chunk, part * CELLS:(part + 1) * CELLS].astype(F32))
            rb[chunk, 2 * part * CELLS:2 * (part + 1) * CELLS] = jnp.concatenate([r1, r2], axis=0)

    def grad_sum(it, part):
        left = jnp.concatenate([rb[chunk, 2 * part * CELLS:2 * (part + 1) * CELLS] for chunk in range(nch)], axis=1)
        right = jnp.concatenate([vst[it, chunk, 0:64] for chunk in range(nch)], axis=1)
        out = lax.dot_general(left, right, (((1,), (1,)), ((), ())), preferred_element_type=F32)
        half = out[0:CELLS] + out[CELLS:2 * CELLS]
        twice = jnp.concatenate([half, half], axis=1)
        g = twice + pltpu.roll(twice, 96, 1)
        quarters = [g[i * rows8:(i + 1) * rows8] for i in range(4)]
        return jnp.where(lanes8 == 0, quarters[0], jnp.where(lanes8 == 1, quarters[1], jnp.where(
            lanes8 == 2, quarters[2], quarters[3])))

    def grad_send(n, part, packed):
        arb[n, part, h] = packed
        send_all("h", lambda i: arb.at[n, part, h], lambda i: arb.at[n, part, i],
                 lambda k: s_ar.at[n, part, k], lambda k: r_ar.at[n, part, k])

    def grad_finish(n, part, u, weights):
        recv_all("h", lambda i: arb.at[n, part, i], lambda k: s_ar.at[n, part, k], lambda k: r_ar.at[n, part, k])
        total = arb[n, part, 0]
        for i in range(1, nh):
            total = total + arb[n, part, i]
        spread = jnp.concatenate([jnp.where(lanes8 == i, total, 0.0) for i in range(4)], axis=0)
        high, low = split2(spread)
        step = jnp.dot(jnp.concatenate([high, low, high], axis=1), weights, preferred_element_type=F32)
        return u - step

    def scatter_start(it, u):
        rows = [x for part in u for x in (part, part)]
        high, low = split2(jnp.concatenate(rows, axis=0).T[0:32])
        lhs = jnp.concatenate([high, low], axis=0)

        whole = jnp.concatenate(u, axis=0)
        square = jnp.where(lax.broadcasted_iota(jnp.int32, (64, 128), 1) < 32, whole * whole, 0.0)
        square = jnp.sum(jnp.sum(square, axis=1, keepdims=True), axis=0, keepdims=True)
        square = jnp.broadcast_to(square, (8, by))

        def make(slot, j):
            out = jnp.dot(lhs, rb[slot * ny + j], preferred_element_type=F32)
            gp[it, slot, j, 0:32] = out[0:32] + out[32:64]
            gp[it, slot, j, 32:40] = square

        copies = []
        for j in range(ny):
            make(1, j)
            copies.append(send_pair(gp.at[it, 1, j], prs.at[it, j], s_rs.at[it, 0, j], r_rs.at[it, 0, j]))
        for j in range(ny):
            make(0, j)
        return copies

    def scatter_first(it, copies):
        for j, copy in enumerate(copies):
            copy.wait_recv()
            gp[it, 0, j] += prs[it, j]
        send_all("y", lambda i: gp.at[it, 0, i, top, :], lambda i: ra1.at[it, i], sem(s_rs, it, 1), sem(r_rs, it, 1))
        send_all("x", lambda i: gp.at[it, 0, :, pl.ds(16, 24), xcols(i)], lambda i: rb1.at[it, i], sem(s_rs, it, 2), sem(r_rs, it, 2))
        ra1[it, y] = gp[it, 0, y, 0:16, :]
        rb1[it, x] = gp[it, 0, :, 16:40, xs]

    def scatter_second(it):
        recv_all("y", lambda i: ra1.at[it, i], sem(s_rs, it, 1), sem(r_rs, it, 1))
        total = ra1[it, 0]
        for i in range(1, ny):
            total = total + ra1[it, i]
        a1[it] = total
        send_all("x", lambda i: a1.at[it, :, xcols(i)], lambda i: ra2.at[it, i], sem(s_rs, it, 3), sem(r_rs, it, 3))
        recv_all("x", lambda i: rb1.at[it, i], sem(s_rs, it, 2), sem(r_rs, it, 2))
        total = rb1[it, 0]
        for i in range(1, nx):
            total = total + rb1[it, i]
        b1[it] = total
        send_all("y", lambda i: b1.at[it, i], lambda i: rb2.at[it, i], sem(s_rs, it, 4), sem(r_rs, it, 4))
        ra2[it, x] = a1[it, :, xs]
        rb2[it, y] = b1[it, y]

    def scatter_third(it):
        recv_all("x", lambda i: ra2.at[it, i], sem(s_rs, it, 3), sem(r_rs, it, 3))
        recv_all("y", lambda i: rb2.at[it, i], sem(s_rs, it, 4), sem(r_rs, it, 4))
        total = ra2[it, 0]
        for i in range(1, nx):
            total = total + ra2[it, i]
        rz[it, z, 0:16] = total
        total = rb2[it, 0]
        for i in range(1, ny):
            total = total + rb2[it, i]
        rz[it, z, 16:40] = total
        send_all("z", lambda i: rz.at[it, z], lambda i: rz.at[it, i], sem(s_rs, it, 5), sem(r_rs, it, 5))

    def scatter_finish(it, gram_trace):
        recv_all("z", lambda i: rz.at[it, i], sem(s_rs, it, 5), sem(r_rs, it, 5))
        total = rz[it, 0]
        for i in range(1, nz):
            total = total + rz[it, i]
        rate = (0.5 * RANK) / total[32:33, 0:1]
        level = 0.1 * jnp.sqrt(gram_trace / (RANK * genes) + 1e-06)
        w = vb[it, 0, y, :, xs] - rate * total[0:32]
        return jnp.where(w > level, w - level, jnp.where(w < -level, w + level, 0.0)) / 1.1

    recv_all("z", lambda i: zbuf.at[i], lambda k: s_z.at[k], lambda k: r_z.at[k])
    for t in range(bx // 128):
        vb[0, 0, y, :, pl.ds(pl.multiple_of(x * bx + t * 128, 128), 128)] = zbuf[2 * t] + zbuf[2 * t + 1]
    gather_first(0)
    pl.semaphore_wait(met_ring, 2)
    for k in range(1, nz):
        signal(met_line, to_z(lax.rem(z + k, nz)))
    for copy in inputs[1:]:
        copy.wait()
    sf = jnp.log(sf_ref[...].astype(F32) / 2000.0)
    sf = jnp.where(core == 0, sf, pltpu.roll(sf, 64, 1))
    o1, o2, o3 = split3(sf)
    offrows = jnp.where(row == 0, o1, jnp.where(row == 1, o2, jnp.where(row == 2, o3, jnp.where(row < 6, 1.0, 0.0))))
    u = jnp.where(core == 0, u_ref[...], pltpu.roll(u_ref[...], 64, 1))
    u = jnp.concatenate([u, u, u, offrows], axis=0).T
    u = [u[part * CELLS:(part + 1) * CELLS] for part in range(PARTS)]
    extra_slot(0, goff_ref)
    pieces = gather_second(0)
    pl.semaphore_wait(met_line, nz - 1)
    sides = sorted({1, nh - 1})
    for k in sides:
        signal(met_far, to_h(lax.rem(h + k, nh)))
    go_copy.wait_recv()
    extra_slot(1, gop)
    for copy in local:
        copy.wait()
    pieces = gather_third(0, pieces)
    stack_slot(0, 0)
    gram_copy = gram_own(0)
    for part in range(PARTS):
        grad_exp(0, part, u[part], 0, ny)
        if part == 0:
            pl.semaphore_wait(met_far, len(sides))
            gram_send(0, gram_copy)
    for copy in cnt_copies + pieces:
        copy.wait_recv()
    stack_slot(0, 1)

    weights = None
    for it in range(ITERS):
        for turn in range(FACTOR_STEPS):
            n = 4 * it + turn
            for part in range(PARTS):
                if n > 0:
                    u[part] = grad_finish(n - 1, part, u[part], weights)
                grad_exp(it, part, u[part], ny if n == 0 else 0, nch)
                grad_send(n, part, grad_sum(it, part))
            if turn == 0:
                copies = scatter_start(it, u)
                scatter_first(it, copies)
                gram_trace, weights = gram_finish(it)
            elif turn == 1:
                scatter_second(it)
                scatter_third(it)
            elif turn == 2:
                fresh = scatter_finish(it, gram_trace)
                if it < ITERS - 1:
                    vb[it + 1, 0, y, :, xs] = fresh
                    gather_first(it + 1)
                    pieces = gather_second(it + 1)
                else:
                    vnew[...] = fresh
                    vo_ref[...] = vnew[:, pl.ds(pl.multiple_of((z // 2) * 128, 128), 128)]
            elif it < ITERS - 1:
                pieces = gather_third(it + 1, pieces)
                stack_slot(it + 1, 0)
                gram_copy = gram_own(it + 1)
                for copy in pieces:
                    copy.wait_recv()
                stack_slot(it + 1, 1)
                gram_send(it + 1, gram_copy)
    copies = []
    for part in range(PARTS):
        u[part] = grad_finish(ITERS * FACTOR_STEPS - 1, part, u[part], weights)
        upb[0, part] = u[part]
        copies.append(send_pair(upb.at[0, part], upb.at[1, part], s_uf.at[part], r_uf.at[part]))
    for copy in copies:
        copy.wait_recv()
    theirs = [upb[1, part] for part in range(PARTS)]
    mine_first = jnp.concatenate(u + theirs, axis=0)
    theirs_first = jnp.concatenate(theirs + u, axis=0)
    uo_ref[...] = jnp.where(core == 0, mine_first, theirs_first).T[0:32]
    for copy in pending:
        copy.wait_send()


def on_device(dims, counts, size_factor, gene_offset, factors, loadings):
    ny, nx, nz, nh = dims
    bx = nz * 64
    by = nx * bx
    slab = ny * by
    nch = 2 * ny
    most = max(ny, nx, nz, nh)
    shard = loadings.reshape(RANK, 64)
    hbm = pl.BlockSpec(memory_space=pltpu.HBM)
    dma = pltpu.SemaphoreType.DMA
    regular = pltpu.SemaphoreType.REGULAR
    vmem = pl.BlockSpec(memory_space=pltpu.VMEM)
    scratch = [
        pltpu.VMEM((1, 128), jnp.int32),
        pltpu.VMEM((1, slab), F32),
        pltpu.VMEM((RANK, 128), F32),
        pltpu.VMEM((RANK, 64), F32),
        pltpu.VMEM((nch, 64, by), jnp.int32),
        pltpu.VMEM((1, slab), F32),
        pltpu.VMEM((nz, RANK, 128), F32),
        pltpu.VMEM((ITERS, 2, ny, RANK, by), F32),
        pltpu.VMEM((ITERS, nch, 128, by), BF16),
        pltpu.VMEM((nch, 128, by), BF16),
        pltpu.VMEM((ITERS, 2, ny, RANK + 8, by), F32),
        pltpu.VMEM((ITERS, ny, RANK + 8, by), F32),
        pltpu.VMEM((ITERS, ny, 16, by), F32),
        pltpu.VMEM((ITERS, nx, ny, 24, bx), F32),
        pltpu.VMEM((ITERS, 16, by), F32),
        pltpu.VMEM((ITERS, ny, 24, bx), F32),
        pltpu.VMEM((ITERS, nx, 16, bx), F32),
        pltpu.VMEM((ITERS, ny, 24, bx), F32),
        pltpu.VMEM((ITERS, nz, RANK + 8, bx), F32),
        pltpu.VMEM((RANK, bx), F32),
        pltpu.VMEM((ITERS * FACTOR_STEPS, PARTS, nh, CELLS // 4, 128), F32),
        pltpu.VMEM((ITERS, nh, 8, 128), F32),
        pltpu.VMEM((ITERS, 2, 8, 128), F32),
        pltpu.VMEM((2, PARTS, CELLS, 128), F32),
        dma((4,)), regular, regular, regular, dma((ITERS,)), dma((ITERS,)),
        dma((ny,)), dma((ny,)), dma((ny,)), dma((1,)), dma((1,)),
        dma((nz,)), dma((nz,)),
        dma((ITERS, 6, most)), dma((ITERS, 6, most)),
        dma((ITERS, 6, most)), dma((ITERS, 6, most)),
        dma((ITERS * FACTOR_STEPS, PARTS, nh)), dma((ITERS * FACTOR_STEPS, PARTS, nh)),
        dma((ITERS, nh)), dma((ITERS, nh)),
        dma((PARTS,)), dma((PARTS,)),
    ]
    u_next, v_next = pl.pallas_call(
        functools.partial(kernel, dims),
        out_shape=(jax.ShapeDtypeStruct((RANK, 128), F32), jax.ShapeDtypeStruct((RANK, 128), F32)),
        in_specs=[hbm] * 5,
        out_specs=(vmem, vmem),
        scratch_shapes=scratch,
        compiler_params=pltpu.CompilerParams(
            collective_id=0, has_side_effects=True, vmem_limit_bytes=48 * 1024 * 1024),
    )(*[pltpu.with_memory_space_constraint(v, pltpu.HBM) for v in (counts, size_factor.reshape(1, 128), gene_offset.reshape(1, slab), factors, shard)])
    odd = lax.rem(lax.axis_index("cell"), 2) == 1
    v_next = jnp.where(odd, v_next[:, 64:], v_next[:, :64])
    return u_next, v_next.reshape(RANK, 1, 64)


def solution(mesh):
    dims = SPLITS[mesh.shape["cell"]] + (mesh.shape["gene"] // 2,)
    return jax.shard_map(
        functools.partial(on_device, dims),
        mesh=mesh,
        in_specs=(
            P("cell", "gene"),
            P("cell"),
            P("gene"),
            P(None, "cell"),
            P(None, "gene", "cell"),
        ),
        out_specs=(P(None, "cell"), P(None, "gene", "cell")),
        check_vma=False,
    )
```
